256 devices in a mesh: grp: 2 (over x_hi), ep: 64 (over x_lo, y, z), dp: 2 (over core).
Axes of the slice: x: 4 (x_hi: 2, x_lo: 2; x = x_hi * 2 + x_lo), y: 4, z: 8, core: 2. Of those that a mesh axis runs over, the one named last changes fastest.
Arguments:
- rows_in: bfloat16 [2, 2048, 4096], P('grp', ('ep', 'dp')), may hold values from -6 to 6
- cotangent: bfloat16 [2048, 4096], P(('ep', 'dp')), may hold values from -6 to 6
- lengths: int32 [4], replicated, may hold values from 1 to 1024, 2048 in all
- train_experts: int32 [2048, 8], P(('ep', 'dp')), may hold values from 0 to 63, all different within a row; in each aligned block of 16 rows (0 to 15, 16 to 31, ...) at most 2 rows name the same one
- train_gates: float32 [2048, 8], P(('ep', 'dp')), may hold values from 0.02 to 0.3
- decode_experts: int32 [2, 2048, 8], P(None, ('ep', 'dp')), may hold values from 0 to 63, all different within a row; in each aligned block of 16 rows (0 to 15, 16 to 31, ..., all dimensions but the last counted through in order) at most 2 rows name the same one
- decode_gates: float32 [2, 2048, 8], P(None, ('ep', 'dp')), may hold values from 0.02 to 0.3
- gate_up: bfloat16 [2, 64, 4096, 2, 768], P('grp', 'ep', None, None, 'dp'), may hold values from -0.09375 to 0.09375
- down: bfloat16 [2, 64, 768, 4096], P('grp', 'ep', 'dp'), may hold values from -0.21875 to 0.21875
Outputs:
- result: bfloat16 [2, 2048, 4096], P('grp', ('ep', 'dp'))
The draws below stay inside these ranges and needn't reach their ends.
Inputs may be any that keep to these rules, and one draw needn't show every extreme that they name: `train_experts`: in every aligned block of 16 rows (the rows of one device), the 8 ids of a row differ and no id is named by more than 2 rows of the block; some block reaches 2. `decode_experts`: for each step, in every aligned block of 16 rows (the rows of one device), the 8 ids of a row differ and no id is named by more than 2 rows of the block; some block reaches 2. The lengths sum to 2048 and the longest is exactly 1024.
All inputs are finite; a program needn't handle non-finite values.
Results may differ from the reference program's by a relative error of at most 0.008.
Values may be sent and summed in bfloat16 or wider, within the bound.
A program may use at most 192 MiB of HBM per device.

```python
import math
import jax
import jax.numpy as jnp
import numpy as np
from jax import lax

D = 4096
HID = 768
TOP = 8
DSTEPS = 2
ROWS_DEV = 16
EXPERTS = 64
NROWS = 2048
CAP = 2
SEQS = 4
MAXLEN = 1024
N_EP = 64
N_DP = 2


def levels(rng, shape, cuts, least, top_value):
    def one(axis_at, parts):
        heights = jax.random.uniform(jax.random.fold_in(jax.random.fold_in(rng, 6), axis_at), (parts,), jnp.float32, least / len(cuts), top_value / len(cuts))
        return jnp.repeat(jnp.exp(heights), shape[axis_at] // parts).reshape((-1,) + (1,) * (len(shape) - axis_at - 1))

    level = one(*cuts[0])
    for cut in cuts[1:]:
        level = level * one(*cut)
    return level


def length_profile(count, total, bound, slope):
    weights = [(1 << 20) // math.isqrt(grade ** slope) + 1 for grade in range(2, count + 1)]
    rest, counts = total - bound - (count - 1), [1] * (count - 1)
    while rest > 0:
        free = [i for i in range(count - 1) if counts[i] < bound]
        mass, left = sum([weights[i] for i in free]), rest
        for i in free:
            addition = min(bound - counts[i], max(1, left * weights[i] // mass), rest)
            counts[i] = counts[i] + addition
            rest = rest - addition
    return np.array([bound] + counts)


def ragged(stream_key, count, total, most, slope):
    if count == 2:
        one = jax.random.randint(stream_key, (), max(1, total - most), min(most, total - 1) + 1)
        return jnp.stack([one, total - one])
    tallies = jnp.asarray(length_profile(count, total, most, slope), jnp.int32)
    twos = (count - 1) // 2
    giver, receiver = tallies[1:1 + 2 * twos:2], tallies[2:2 + 2 * twos:2]
    room = jnp.minimum(giver - 1, most - receiver)
    shifted = jax.random.randint(jax.random.fold_in(stream_key, 1), (twos,), 0, 1 << 20) % (room + 1)
    tallies = tallies.at[1:1 + 2 * twos:2].set(giver - shifted).at[2:2 + 2 * twos:2].set(receiver + shifted)
    return tallies[jax.random.permutation(jax.random.fold_in(stream_key, 2), count)]


def assign_block(stream_key, own, number, rows, number_of, top, reach, skew):
    order = jax.random.permutation(stream_key, number_of)
    crowded, usual = shares(number_of, rows * top, reach, skew, True), shares(number_of, rows * top, reach, skew, False)
    places = jnp.arange(number_of)

    def named(tallies, offset_by):
        used = int((tallies > 0).sum())
        fixed = max(1, used // 4)
        moved = fixed + (places - fixed + offset_by * (used - fixed)) % max(1, number_of - fixed)
        return jnp.zeros((number_of,), jnp.int32).at[order[jnp.where(places < fixed, places, moved)]].set(jnp.asarray(tallies, jnp.int32))

    tallies = jnp.where(number % 4 == 0, named(crowded, number // 4), named(usual, number - number // 4 - 1))
    mixed = jax.random.permutation(jax.random.fold_in(own, 3), number_of)
    source_of, sink = mixed[0:number_of // 2 * 2:2], mixed[1:number_of // 2 * 2:2]
    slack = jnp.minimum(tallies[source_of] - 1, reach - tallies[sink]) // 2
    slack = jnp.where((source_of == order[0]) | (sink == order[0]) | (tallies[sink] == 0), 0, jnp.maximum(slack, 0))
    moved = jax.random.randint(jax.random.fold_in(own, 4), (number_of // 2,), 0, 1 << 20) % (slack + 1)
    tallies = tallies.at[source_of].add(-moved).at[sink].add(moved)
    items = jnp.searchsorted(jnp.cumsum(tallies), jnp.arange(rows * top), side="right").astype(jnp.int32)
    listing = items.reshape(top, rows).T
    listing = listing[jax.random.permutation(jax.random.fold_in(own, 1), rows)]
    offset_by = jax.random.randint(jax.random.fold_in(own, 2), (rows, 1), 0, top)
    return jnp.take_along_axis(listing, (jnp.arange(top)[None, :] + offset_by) % top, axis=1)


def shares(number_of, total, reach, skew, full):
    portions = [(1 << 20) // math.isqrt(standing ** skew) + 1 for standing in range(1, number_of + 1)]
    largest = reach if full else min(reach, max(-(-total // number_of), total * portions[0] // sum(portions)))
    least = 1 if total - largest >= number_of - 1 else 0
    counts, rest = [largest] + [least] * (number_of - 1), total - largest - least * (number_of - 1)
    while rest > 0:
        candidates = [i for i in range(1, number_of) if counts[i] < largest] or [i for i in range(1, number_of) if counts[i] < reach]
        whole, remaining = sum([portions[i] for i in candidates]), rest
        for i in candidates:
            extra = min(reach - counts[i], max(1, remaining * portions[i] // whole), rest)
            counts[i] = counts[i] + extra
            rest = rest - extra
    return np.array(counts)


def centred(stream_key, dims, scale, bound, shards=(), held_as=jnp.bfloat16):
    array = scale * jax.random.normal(stream_key, dims, jnp.float32)
    if shards:
        array = array * levels(stream_key, dims, shards, -0.22, 0.18)
    return jnp.clip(array, -bound, bound).astype(held_as)


def setup_inputs(seed: int = 0) -> dict:
    key_of = jax.random.split(jax.random.key(seed), 10)
    rows_in = centred(key_of[0], (2, NROWS, D), 1.0, 6.0, ((0, 2), (1, 128)))
    cotangent = centred(key_of[1], (NROWS, D), 1.0, 6.0, ((0, 128),))
    lengths = ragged(key_of[2], SEQS, NROWS, MAXLEN, 2).astype(jnp.int32)
    train_experts_keys = jax.random.split(jax.random.fold_in(key_of[3], 1), NROWS // ROWS_DEV)
    train_experts_turns = jax.random.permutation(jax.random.fold_in(key_of[3], 3), NROWS // ROWS_DEV)
    train_experts = jax.vmap(lambda own, number: assign_block(jax.random.fold_in(key_of[3], 2), own, number, ROWS_DEV, EXPERTS, TOP, CAP, 2))(train_experts_keys, train_experts_turns).reshape((NROWS, TOP))
    train_gates = jnp.clip(0.02 + 0.28 * jax.random.uniform(key_of[4], (NROWS, TOP), jnp.float32) ** levels(key_of[4], (NROWS, TOP), ((0, 128),), -0.2, 0.2), 0.02, 0.3)
    decode_experts_keys = jax.random.split(jax.random.fold_in(key_of[5], 1), DSTEPS * NROWS // ROWS_DEV)
    decode_experts_turns = jax.random.permutation(jax.random.fold_in(key_of[5], 3), DSTEPS * NROWS // ROWS_DEV)
    decode_experts = jax.vmap(lambda own, number: assign_block(jax.random.fold_in(key_of[5], 2), own, number, ROWS_DEV, EXPERTS, TOP, CAP, 2))(decode_experts_keys, decode_experts_turns).reshape((DSTEPS, NROWS, TOP))
    decode_gates = jnp.clip(0.02 + 0.28 * jax.random.uniform(key_of[6], (DSTEPS, NROWS, TOP), jnp.float32) ** levels(key_of[6], (DSTEPS, NROWS, TOP), ((1, 128),), -0.2, 0.2), 0.02, 0.3)
    gate_up = centred(key_of[7], (2, EXPERTS, D, 2, HID), D ** -0.5, 0.09375, ((0, 2), (1, 64), (4, 2)))
    down = centred(key_of[8], (2, EXPERTS, HID, D), HID ** -0.5, 0.21875, ((0, 2), (1, 64), (2, 2)))
    return {"rows_in": rows_in, "cotangent": cotangent, "lengths": lengths, "train_experts": train_experts, "train_gates": train_gates, "decode_experts": decode_experts, "decode_gates": decode_gates, "gate_up": gate_up, "down": down}


EPSILON = 1e-06

def round_keep(values):
    return lax.optimization_barrier(values.astype(jnp.bfloat16)).astype(jnp.float32)

def token_weights(lengths):
    ends = jnp.cumsum(lengths).astype(jnp.int32)
    starts = ends - lengths
    places = jnp.arange(NROWS, dtype=jnp.int32)
    inside = (places[:, None] >= starts[None, :]) & (places[:, None] < ends[None, :])
    seq_len = lax.optimization_barrier(jnp.sum(jnp.where(inside, lengths[None, :], 0), axis=1)).astype(jnp.float32)
    return 2.0 * MAXLEN / (seq_len + MAXLEN)

def slot_tables(expert_ids):
    blocks = expert_ids.reshape(N_EP * N_DP, ROWS_DEV * TOP)
    onehot = (blocks[:, :, None] == jnp.arange(EXPERTS, dtype=jnp.int32)[None, None, :]).astype(jnp.int32)
    ranks = lax.optimization_barrier(jnp.sum((jnp.cumsum(onehot, axis=1) - onehot) * onehot, axis=2))
    sources = jnp.arange(N_EP * N_DP, dtype=jnp.int32)[:, None]
    position = (sources * CAP + ranks).reshape(-1).astype(jnp.int32)
    expert = expert_ids.reshape(-1).astype(jnp.int32)
    pairs = jnp.arange(NROWS * TOP, dtype=jnp.int32)
    table = jnp.full((EXPERTS, N_EP * N_DP * CAP), NROWS * TOP, jnp.int32).at[expert, position].set(pairs)
    return (table, expert, position)

def expert_forward(slot_rows, weights_gu, weights_dn):
    both = jnp.dot(slot_rows, weights_gu.reshape(D, 2 * HID), preferred_element_type=jnp.float32).reshape(-1, 2, HID)
    active = both[:, 0]
    upward = both[:, 1]
    hidden = (active * jax.nn.sigmoid(active) * upward).astype(jnp.bfloat16)
    part_size = HID // N_DP
    total = jnp.zeros((slot_rows.shape[0], D), jnp.float32)
    for part_index in range(N_DP):
        lower = part_index * part_size
        piece = jnp.dot(hidden[:, lower:lower + part_size], weights_dn[lower:lower + part_size], preferred_element_type=jnp.float32)
        total = total + round_keep(piece)
    return total

def expert_learn(slot_rows, slot_grads, weights_gu, weights_dn):
    count = N_EP * N_DP * CAP
    both = jnp.dot(slot_rows, weights_gu.reshape(D, 2 * HID), preferred_element_type=jnp.float32).reshape(count, 2, HID)
    active = both[:, 0]
    upward = both[:, 1]
    sigma = jax.nn.sigmoid(active)
    swish = active * sigma
    hidden = (swish * upward).astype(jnp.bfloat16)
    back = lax.dot_general(slot_grads, weights_dn, (((1,), (1,)), ((), ())), preferred_element_type=jnp.float32)
    d_active = back * upward * sigma * (1.0 + active * (1.0 - sigma))
    d_upward = back * swish
    d_both = jnp.stack([d_active, d_upward], axis=1).astype(jnp.bfloat16)
    rows_four = slot_rows.reshape(N_EP, N_DP, CAP, D).astype(jnp.float32)
    grads_four = slot_grads.reshape(N_EP, N_DP, CAP, D).astype(jnp.float32)
    per_dn = jnp.einsum('epch,epcd->phd', hidden.reshape(N_EP, N_DP, CAP, HID).astype(jnp.float32), grads_four, precision=lax.Precision.HIGHEST)
    per_gu = jnp.einsum('epcd,epcgh->pdgh', rows_four, d_both.reshape(N_EP, N_DP, CAP, 2, HID).astype(jnp.float32), precision=lax.Precision.HIGHEST)
    grad_dn = jnp.zeros((HID, D), jnp.float32)
    grad_gu = jnp.zeros((D, 2, HID), jnp.float32)
    for replica in range(N_DP):
        grad_dn = grad_dn + round_keep(per_dn[replica])
        grad_gu = grad_gu + round_keep(per_gu[replica])
    part_size = HID // N_DP
    slot_dx = jnp.zeros((count, D), jnp.float32)
    for part_index in range(N_DP):
        lower = part_index * part_size
        piece = jnp.einsum('mgh,dgh->md', d_both[:, :, lower:lower + part_size].astype(jnp.float32), weights_gu[:, :, lower:lower + part_size].astype(jnp.float32), precision=lax.Precision.HIGHEST)
        slot_dx = slot_dx + round_keep(piece)
    scale_gu = jnp.sqrt(lax.optimization_barrier(jnp.mean(grad_gu * grad_gu, axis=0, keepdims=True)) + EPSILON)
    scale_dn = jnp.sqrt(lax.optimization_barrier(jnp.mean(grad_dn * grad_dn, axis=1, keepdims=True)) + EPSILON)
    fresh_gu = (weights_gu.astype(jnp.float32) - 0.5 / D ** 0.5 * grad_gu / scale_gu).astype(jnp.bfloat16)
    fresh_dn = (weights_dn.astype(jnp.float32) - 0.5 / HID ** 0.5 * grad_dn / scale_dn).astype(jnp.bfloat16)
    return (slot_dx, fresh_gu, fresh_dn)

def reference(rows_in, cotangent, lengths, train_experts, train_gates, decode_experts, decode_gates, gate_up, down):
    weight = token_weights(lengths)
    zero_row = jnp.zeros((1, D), jnp.bfloat16)
    tokens = jnp.concatenate([rows_in[0], zero_row], axis=0)
    cot_pad = jnp.concatenate([cotangent, zero_row], axis=0)
    scaled = (train_gates * weight[:, None]).reshape(-1)
    scale_pad = jnp.concatenate([scaled, jnp.zeros((1,), jnp.float32)], axis=0)
    learn_table, learn_expert, learn_position = slot_tables(train_experts)

    def stale_step(current, step_index):
        table, expert, position = slot_tables(decode_experts[step_index])
        padded = jnp.concatenate([current, zero_row], axis=0)

        def one_expert(expert_index):
            return expert_forward(padded[table[expert_index] // TOP], gate_up[1, expert_index], down[1, expert_index])
        outputs = lax.map(one_expert, jnp.arange(EXPERTS, dtype=jnp.int32))
        pair_out = outputs[expert, position].reshape(NROWS, TOP, D)
        added = lax.optimization_barrier(jnp.sum(decode_gates[step_index][:, :, None] * pair_out, axis=1))
        return (current.astype(jnp.float32) + added).astype(jnp.bfloat16)

    def fresh_step(current, step_index):
        table, expert, position = slot_tables(decode_experts[step_index])
        padded = jnp.concatenate([current, zero_row], axis=0)

        def one_expert(expert_index):
            slot_pairs = learn_table[expert_index]
            slot_rows = tokens[slot_pairs // TOP]
            slot_grads = (scale_pad[slot_pairs][:, None] * cot_pad[slot_pairs // TOP].astype(jnp.float32)).astype(jnp.bfloat16)
            slot_dx, fresh_gu, fresh_dn = expert_learn(slot_rows, slot_grads, gate_up[0, expert_index], down[0, expert_index])
            return (slot_dx, expert_forward(padded[table[expert_index] // TOP], fresh_gu, fresh_dn))
        dx_slots, outputs = lax.map(one_expert, jnp.arange(EXPERTS, dtype=jnp.int32))
        pair_out = outputs[expert, position].reshape(NROWS, TOP, D)
        added = lax.optimization_barrier(jnp.sum(decode_gates[step_index][:, :, None] * pair_out, axis=1))
        return ((current.astype(jnp.float32) + added).astype(jnp.bfloat16), dx_slots)
    current = stale_step(rows_in[1], 0)
    current, dx_slots = fresh_step(current, 1)
    for step_index in range(2, DSTEPS):
        current, ignored = fresh_step(current, step_index)
    pair_dx = dx_slots[learn_expert, learn_position].reshape(NROWS, TOP, D)
    grads = weight[:, None] * cotangent.astype(jnp.float32) + lax.optimization_barrier(jnp.sum(pair_dx, axis=1))
    return jnp.stack([grads.astype(jnp.bfloat16), current], axis=0)
```

```python
import jax
import jax.numpy as jnp
from jax import lax
from jax.sharding import PartitionSpec as P

EPSILON = 1e-06


def passed_along(block, axis, distance):
    devices = range(lax.axis_size(axis))
    route = [(i - distance, i) for i in devices if i - distance in devices]
    return lax.ppermute(block, axis, route)


def routing_tables(expert_ids, gate_values, capacity, expert_count):
    row_count, top_count = expert_ids.shape
    flat_ids = expert_ids.reshape(row_count * top_count)
    onehot = (flat_ids[:, None] == jnp.arange(expert_count, dtype=jnp.int32)[None, :]).astype(
        jnp.int32
    )
    earlier = jnp.cumsum(onehot, axis=0) - onehot
    ranks = jnp.sum(earlier * onehot, axis=1)
    slots = flat_ids * capacity + ranks
    hits = (slots[:, None] == jnp.arange(expert_count * capacity, dtype=jnp.int32)[None, :]).astype(
        jnp.float32
    )
    hits = hits.reshape(row_count, top_count, expert_count * capacity)
    picker = jnp.sum(hits, axis=1)
    weigher = jnp.sum(hits * gate_values[:, :, None], axis=1)
    return (picker, weigher)


def replica_sum(per_replica):
    total = jnp.zeros(per_replica.shape[1:], jnp.float32)
    for replica in range(per_replica.shape[0]):
        total = total + lax.optimization_barrier(per_replica[replica].astype(jnp.bfloat16)).astype(
            jnp.float32
        )
    return total


def renew(weights, grads, axis_number, rate):
    scale = jnp.sqrt(jnp.mean(grads * grads, axis=axis_number, keepdims=True) + EPSILON)
    return (weights.astype(jnp.float32) - rate * grads / scale).astype(jnp.bfloat16)


def forward_core(rows_four, weights_gu, weights_dn, part_count):
    ep_count, rep_count, capacity, model_width = rows_four.shape
    hidden_count = weights_gu.shape[2]
    slot_count = ep_count * rep_count * capacity
    both = jnp.dot(
        rows_four.reshape(slot_count, model_width),
        weights_gu.reshape(model_width, 2 * hidden_count),
        preferred_element_type=jnp.float32,
    ).reshape(slot_count, 2, hidden_count)
    active = both[:, 0]
    upward = both[:, 1]
    hidden = (active * jax.nn.sigmoid(active) * upward).astype(jnp.bfloat16)
    piece = jnp.dot(hidden, weights_dn, preferred_element_type=jnp.float32)
    pieces = piece.astype(jnp.bfloat16).reshape(ep_count, rep_count, 1, capacity, model_width)
    return pieces.reshape(ep_count, rep_count * part_count, capacity, model_width)


def learn_core(rows_four, grads_four, weights_gu, weights_dn, part_count):
    ep_count, rep_count, capacity, model_width = rows_four.shape
    hidden_count = weights_gu.shape[2]
    slot_count = ep_count * rep_count * capacity
    flat_grads = grads_four.reshape(slot_count, model_width)
    both = jnp.dot(
        rows_four.reshape(slot_count, model_width),
        weights_gu.reshape(model_width, 2 * hidden_count),
        preferred_element_type=jnp.float32,
    ).reshape(slot_count, 2, hidden_count)
    active = both[:, 0]
    upward = both[:, 1]
    sigma = jax.nn.sigmoid(active)
    swish = active * sigma
    hidden = (swish * upward).astype(jnp.bfloat16)
    back = lax.dot_general(
        flat_grads, weights_dn, (((1,), (1,)), ((), ())), preferred_element_type=jnp.float32
    )
    d_active = back * upward * sigma * (1.0 + active * (1.0 - sigma))
    d_upward = back * swish
    d_both = jnp.stack([d_active, d_upward], axis=1).astype(jnp.bfloat16)
    grad_dn = jnp.einsum(
        "epch,epcd->phd",
        hidden.reshape(ep_count, rep_count, capacity, hidden_count),
        grads_four,
        preferred_element_type=jnp.float32,
    )
    grad_gu = jnp.einsum(
        "epcd,epcgh->pdgh",
        rows_four,
        d_both.reshape(ep_count, rep_count, capacity, 2, hidden_count),
        preferred_element_type=jnp.float32,
    )
    piece = jnp.einsum("mgh,dgh->md", d_both, weights_gu, preferred_element_type=jnp.float32)
    pieces = piece.astype(jnp.bfloat16).reshape(ep_count, rep_count, 1, capacity, model_width)
    ahead = jnp.dot(hidden, weights_dn, preferred_element_type=jnp.float32)
    forward_pieces = ahead.astype(jnp.bfloat16).reshape(
        ep_count, rep_count, 1, capacity, model_width
    )
    slot_dx = pieces.reshape(ep_count, rep_count * part_count, capacity, model_width)
    slot_fw = forward_pieces.reshape(ep_count, rep_count * part_count, capacity, model_width)
    return (grad_gu, grad_dn, slot_dx, slot_fw)


def per_device(
    rows_in,
    cotangent,
    lengths,
    train_experts,
    train_gates,
    decode_experts,
    decode_gates,
    gate_up,
    down,
):
    ep_count = lax.axis_size("ep")
    dp_count = lax.axis_size("dp")
    row_count, model_width = cotangent.shape
    top_count = train_experts.shape[1]
    capacity = min(row_count, max(2, 4 * row_count * top_count // (3 * ep_count)))
    is_learner = lax.axis_index("grp") == 0
    own_gu = gate_up[0, 0]
    own_dn = down[0, 0]
    hidden_all = own_gu.shape[2] * dp_count

    def spread(stacked):
        layers = stacked.shape[0]
        copies = jnp.broadcast_to(
            stacked[:, :, None], (layers, ep_count, dp_count, capacity, model_width)
        )
        copies = copies.reshape(layers, ep_count * dp_count, capacity, model_width)
        arrived = lax.all_to_all(copies, ("ep", "dp"), split_axis=1, concat_axis=1, tiled=True)
        return arrived.reshape(layers, ep_count, dp_count, capacity, model_width)

    def weights_for(weights_gu, weights_dn):
        return (weights_gu, weights_dn, 1)

    def bring_back(slot_out):
        flat_out = slot_out.reshape(ep_count * dp_count, capacity, model_width)
        returned = lax.all_to_all(flat_out, ("ep", "dp"), split_axis=0, concat_axis=0, tiled=True)
        return returned.reshape(ep_count, dp_count, capacity, model_width)

    def combine(mixing, returned):
        total = jnp.sum(returned.astype(jnp.float32), axis=1).reshape(
            ep_count * capacity, model_width
        )
        return jnp.einsum("rs,sd->rd", mixing, total, precision=lax.Precision.HIGHEST)

    def dispatch(picker, values):
        buffer = jnp.einsum(
            "rs,rd->sd", picker.astype(jnp.bfloat16), values, preferred_element_type=jnp.float32
        )
        return buffer.astype(jnp.bfloat16)

    tokens = rows_in[0]
    total_rows = row_count * ep_count * dp_count
    longest = 2 * total_rows // lengths.shape[0]
    first_row = (lax.axis_index("ep") * dp_count + lax.axis_index("dp")) * row_count
    places = first_row + jnp.arange(row_count, dtype=jnp.int32)
    ends = jnp.cumsum(lengths)
    starts = ends - lengths
    inside = (places[:, None] >= starts[None, :]) & (places[:, None] < ends[None, :])
    seq_len = jnp.sum(jnp.where(inside, lengths[None, :], 0), axis=1).astype(jnp.float32)
    weight = 2.0 * longest / (seq_len + longest)
    route_ids = jnp.where(is_learner, train_experts, decode_experts[0])
    route_gates = jnp.where(is_learner, train_gates, decode_gates[0])
    picker, weigher = routing_tables(route_ids, route_gates, capacity, ep_count)
    row_buffer = dispatch(picker, tokens)
    cot_wide = cotangent.astype(jnp.float32)
    grad_buffer = jnp.einsum(
        "rs,rd->sd", weigher * weight[:, None], cot_wide, precision=lax.Precision.HIGHEST
    ).astype(jnp.bfloat16)
    stacked = jnp.stack([row_buffer, grad_buffer], axis=0).reshape(
        2, ep_count, capacity, model_width
    )
    arrived = spread(stacked)
    use_gu, use_dn, part_count = weights_for(own_gu, own_dn)
    per_gu, per_dn, slot_dx, slot_fw = learn_core(
        arrived[0], arrived[1], use_gu, use_dn, part_count
    )
    grad_gu = replica_sum(per_gu)
    grad_dn = replica_sum(per_dn)
    returned = bring_back(jnp.where(is_learner, slot_dx, slot_fw))
    mixing = jnp.where(is_learner, picker, weigher)
    base = jnp.where(is_learner, weight[:, None] * cot_wide, tokens.astype(jnp.float32))
    carried = (base + combine(mixing, returned)).astype(jnp.bfloat16)
    sent_gu = renew(own_gu, grad_gu, 0, 0.5 / model_width**0.5)
    sent_dn = renew(own_dn, grad_dn, 1, 0.5 / hidden_all**0.5)
    fresh_gu, fresh_dn = sent_gu, sent_dn
    current = passed_along(carried, "grp", -1)
    picker, weigher = routing_tables(decode_experts[1], decode_gates[1], capacity, ep_count)
    stacked = dispatch(picker, current).reshape(1, ep_count, capacity, model_width)
    arrived = spread(stacked)
    use_gu, use_dn, part_count = weights_for(fresh_gu, fresh_dn)
    slot_out = forward_core(arrived[0], use_gu, use_dn, part_count)
    returned = bring_back(slot_out)
    current = (current.astype(jnp.float32) + combine(weigher, returned)).astype(jnp.bfloat16)
    final_rows = jnp.where(is_learner, carried, passed_along(current, "grp", 1))
    return final_rows[None]


def solution(mesh):
    placed = (
        P("grp", ("ep", "dp"), None),
        P(("ep", "dp"), None),
        P(),
        P(("ep", "dp"), None),
        P(("ep", "dp"), None),
        P(None, ("ep", "dp"), None),
        P(None, ("ep", "dp"), None),
        P("grp", "ep", None, None, "dp"),
        P("grp", "ep", "dp", None),
    )
    return jax.shard_map(
        per_device,
        mesh=mesh,
        in_specs=placed,
        out_specs=P("grp", ("ep", "dp"), None),
        check_vma=False,
    )
```

```python
import jax
import jax.numpy as jnp
from jax import lax
from jax.sharding import PartitionSpec as P

EPSILON = 1e-06


def passed_along(block, axis, distance):
    devices = range(lax.axis_size(axis))
    route = [(i - distance, i) for i in devices if i - distance in devices]
    return lax.ppermute(block, axis, route)


def routing_tables(expert_ids, gate_values, capacity, expert_count):
    row_count, top_count = expert_ids.shape
    flat_ids = expert_ids.reshape(row_count * top_count)
    onehot = (flat_ids[:, None] == jnp.arange(expert_count, dtype=jnp.int32)[None, :]).astype(
        jnp.int32
    )
    earlier = jnp.cumsum(onehot, axis=0) - onehot
    ranks = jnp.sum(earlier * onehot, axis=1)
    slots = flat_ids * capacity + ranks
    hits = (slots[:, None] == jnp.arange(expert_count * capacity, dtype=jnp.int32)[None, :]).astype(
        jnp.float32
    )
    hits = hits.reshape(row_count, top_count, expert_count * capacity)
    picker = jnp.sum(hits, axis=1)
    weigher = jnp.sum(hits * gate_values[:, :, None], axis=1)
    return (picker, weigher)


def replica_sum(per_replica):
    total = jnp.zeros(per_replica.shape[1:], jnp.float32)
    for replica in range(per_replica.shape[0]):
        total = total + lax.optimization_barrier(per_replica[replica].astype(jnp.bfloat16)).astype(
            jnp.float32
        )
    return total


def renew(weights, grads, axis_number, rate):
    scale = jnp.sqrt(jnp.mean(grads * grads, axis=axis_number, keepdims=True) + EPSILON)
    return (weights.astype(jnp.float32) - rate * grads / scale).astype(jnp.bfloat16)


def forward_core(rows_four, weights_gu, weights_dn, part_count):
    ep_count, rep_count, capacity, model_width = rows_four.shape
    hidden_count = weights_gu.shape[2]
    slot_count = ep_count * rep_count * capacity
    both = jnp.dot(
        rows_four.reshape(slot_count, model_width),
        weights_gu.reshape(model_width, 2 * hidden_count),
        preferred_element_type=jnp.float32,
    ).reshape(slot_count, 2, hidden_count)
    active = both[:, 0]
    upward = both[:, 1]
    hidden = (active * jax.nn.sigmoid(active) * upward).astype(jnp.bfloat16)
    piece = jnp.dot(hidden, weights_dn, preferred_element_type=jnp.float32)
    pieces = piece.astype(jnp.bfloat16).reshape(ep_count, rep_count, 1, capacity, model_width)
    return pieces.reshape(ep_count, rep_count * part_count, capacity, model_width)


def learn_core(rows_four, grads_four, weights_gu, weights_dn, part_count):
    ep_count, rep_count, capacity, model_width = rows_four.shape
    hidden_count = weights_gu.shape[2]
    slot_count = ep_count * rep_count * capacity
    flat_grads = grads_four.reshape(slot_count, model_width)
    both = jnp.dot(
        rows_four.reshape(slot_count, model_width),
        weights_gu.reshape(model_width, 2 * hidden_count),
        preferred_element_type=jnp.float32,
    ).reshape(slot_count, 2, hidden_count)
    active = both[:, 0]
    upward = both[:, 1]
    sigma = jax.nn.sigmoid(active)
    swish = active * sigma
    hidden = (swish * upward).astype(jnp.bfloat16)
    back = lax.dot_general(
        flat_grads, weights_dn, (((1,), (1,)), ((), ())), preferred_element_type=jnp.float32
    )
    d_active = back * upward * sigma * (1.0 + active * (1.0 - sigma))
    d_upward = back * swish
    d_both = jnp.stack([d_active, d_upward], axis=1).astype(jnp.bfloat16)
    grad_dn = jnp.einsum(
        "epch,epcd->phd",
        hidden.reshape(ep_count, rep_count, capacity, hidden_count),
        grads_four,
        preferred_element_type=jnp.float32,
    )
    grad_gu = jnp.einsum(
        "epcd,epcgh->pdgh",
        rows_four,
        d_both.reshape(ep_count, rep_count, capacity, 2, hidden_count),
        preferred_element_type=jnp.float32,
    )
    piece = jnp.einsum("mgh,dgh->md", d_both, weights_gu, preferred_element_type=jnp.float32)
    pieces = piece.astype(jnp.bfloat16).reshape(ep_count, rep_count, 1, capacity, model_width)
    ahead = jnp.dot(hidden, weights_dn, preferred_element_type=jnp.float32)
    forward_pieces = ahead.astype(jnp.bfloat16).reshape(
        ep_count, rep_count, 1, capacity, model_width
    )
    slot_dx = pieces.reshape(ep_count, rep_count * part_count, capacity, model_width)
    slot_fw = forward_pieces.reshape(ep_count, rep_count * part_count, capacity, model_width)
    return (grad_gu, grad_dn, slot_dx, slot_fw)


def per_device(
    rows_in,
    cotangent,
    lengths,
    train_experts,
    train_gates,
    decode_experts,
    decode_gates,
    gate_up,
    down,
):
    ep_count = lax.axis_size("ep")
    dp_count = lax.axis_size("dp")
    row_count, model_width = cotangent.shape
    top_count = train_experts.shape[1]
    capacity = min(row_count, max(2, 4 * row_count * top_count // (3 * ep_count)))
    is_learner = lax.axis_index("grp") == 0
    own_gu = gate_up[0, 0]
    own_dn = down[0, 0]
    hidden_all = own_gu.shape[2] * dp_count

    def spread(stacked):
        arrived = lax.all_to_all(stacked, "ep", split_axis=1, concat_axis=1, tiled=True)
        return lax.all_gather(arrived, "dp", axis=2)

    def weights_for(weights_gu, weights_dn):
        return (weights_gu, weights_dn, 1)

    def bring_back(slot_out):
        mine = lax.axis_index("dp")
        keep = lax.dynamic_index_in_dim(slot_out, mine, axis=1, keepdims=False)
        give = lax.dynamic_index_in_dim(slot_out, 1 - mine, axis=1, keepdims=False)
        got = lax.ppermute(give, "dp", [(0, 1), (1, 0)])
        summed = (keep.astype(jnp.float32) + got.astype(jnp.float32)).astype(jnp.bfloat16)
        return lax.all_to_all(summed, "ep", split_axis=0, concat_axis=0, tiled=True)

    def combine(mixing, returned):
        total = returned.astype(jnp.float32).reshape(ep_count * capacity, model_width)
        return jnp.einsum("rs,sd->rd", mixing, total, precision=lax.Precision.HIGHEST)

    def dispatch(picker, values):
        buffer = jnp.einsum(
            "rs,rd->sd", picker.astype(jnp.bfloat16), values, preferred_element_type=jnp.float32
        )
        return buffer.astype(jnp.bfloat16)

    tokens = rows_in[0]
    total_rows = row_count * ep_count * dp_count
    longest = 2 * total_rows // lengths.shape[0]
    first_row = (lax.axis_index("ep") * dp_count + lax.axis_index("dp")) * row_count
    places = first_row + jnp.arange(row_count, dtype=jnp.int32)
    ends = jnp.cumsum(lengths)
    starts = ends - lengths
    inside = (places[:, None] >= starts[None, :]) & (places[:, None] < ends[None, :])
    seq_len = jnp.sum(jnp.where(inside, lengths[None, :], 0), axis=1).astype(jnp.float32)
    weight = 2.0 * longest / (seq_len + longest)
    route_ids = jnp.where(is_learner, train_experts, decode_experts[0])
    route_gates = jnp.where(is_learner, train_gates, decode_gates[0])
    picker, weigher = routing_tables(route_ids, route_gates, capacity, ep_count)
    row_buffer = dispatch(picker, tokens)
    cot_wide = cotangent.astype(jnp.float32)
    grad_buffer = jnp.einsum(
        "rs,rd->sd", weigher * weight[:, None], cot_wide, precision=lax.Precision.HIGHEST
    ).astype(jnp.bfloat16)
    stacked = jnp.stack([row_buffer, grad_buffer], axis=0).reshape(
        2, ep_count, capacity, model_width
    )
    arrived = spread(stacked)
    use_gu, use_dn, part_count = weights_for(own_gu, own_dn)
    per_gu, per_dn, slot_dx, slot_fw = learn_core(
        arrived[0], arrived[1], use_gu, use_dn, part_count
    )
    grad_gu = replica_sum(per_gu)
    grad_dn = replica_sum(per_dn)
    returned = bring_back(jnp.where(is_learner, slot_dx, slot_fw))
    mixing = jnp.where(is_learner, picker, weigher)
    base = jnp.where(is_learner, weight[:, None] * cot_wide, tokens.astype(jnp.float32))
    carried = (base + combine(mixing, returned)).astype(jnp.bfloat16)
    sent_gu = renew(own_gu, grad_gu, 0, 0.5 / model_width**0.5)
    sent_dn = renew(own_dn, grad_dn, 1, 0.5 / hidden_all**0.5)
    fresh_gu, fresh_dn = sent_gu, sent_dn
    current = passed_along(carried, "grp", -1)
    picker, weigher = routing_tables(decode_experts[1], decode_gates[1], capacity, ep_count)
    stacked = dispatch(picker, current).reshape(1, ep_count, capacity, model_width)
    arrived = spread(stacked)
    use_gu, use_dn, part_count = weights_for(fresh_gu, fresh_dn)
    slot_out = forward_core(arrived[0], use_gu, use_dn, part_count)
    returned = bring_back(slot_out)
    current = (current.astype(jnp.float32) + combine(weigher, returned)).astype(jnp.bfloat16)
    final_rows = jnp.where(is_learner, carried, passed_along(current, "grp", 1))
    return final_rows[None]


def solution(mesh):
    placed = (
        P("grp", ("ep", "dp"), None),
        P(("ep", "dp"), None),
        P(),
        P(("ep", "dp"), None),
        P(("ep", "dp"), None),
        P(None, ("ep", "dp"), None),
        P(None, ("ep", "dp"), None),
        P("grp", "ep", None, None, "dp"),
        P("grp", "ep", "dp", None),
    )
    return jax.shard_map(
        per_device,
        mesh=mesh,
        in_specs=placed,
        out_specs=P("grp", ("ep", "dp"), None),
        check_vma=False,
    )
```

```python
import jax
import jax.numpy as jnp
from jax import lax
from jax.experimental import pallas as pl
from jax.experimental.pallas import tpu as pltpu
from jax.sharding import PartitionSpec as P
import functools

MESH = pl.DeviceIdType.MESH


def exchange_kernel(count, x_ref, y_ref, send_sem, recv_sem, own_sem):
    me = lax.axis_index("ep")
    barrier = pltpu.get_barrier_semaphore()

    def greet(k, carry):
        other = lax.rem(me + k, count)
        pl.semaphore_signal(barrier, inc=1, device_id={"ep": other}, device_id_type=MESH)
        return carry

    lax.fori_loop(1, count, greet, 0)
    pl.semaphore_wait(barrier, count - 1)
    own = pltpu.make_async_copy(x_ref.at[me], y_ref.at[me], own_sem)
    own.start()

    def outgoing(k):
        other = lax.rem(me + k, count)
        return pltpu.make_async_remote_copy(
            src_ref=x_ref.at[other],
            dst_ref=y_ref.at[me],
            send_sem=send_sem.at[other],
            recv_sem=recv_sem.at[me],
            device_id={"ep": other},
            device_id_type=MESH,
        )

    def incoming(k):
        other = lax.rem(me + count - k, count)
        return pltpu.make_async_remote_copy(
            src_ref=x_ref.at[other],
            dst_ref=y_ref.at[other],
            send_sem=send_sem.at[other],
            recv_sem=recv_sem.at[other],
            device_id={"ep": other},
            device_id_type=MESH,
        )

    def launch(k, carry):
        outgoing(k).start()
        return carry

    lax.fori_loop(1, count, launch, 0)

    def settle(k, carry):
        outgoing(k).wait_send()
        return carry

    lax.fori_loop(1, count, settle, 0)

    def land(k, carry):
        incoming(k).wait_recv()
        return carry

    lax.fori_loop(1, count, land, 0)
    own.wait()


def exchange(x, tag):
    count = x.shape[0]
    size = x.size * x.dtype.itemsize
    return pl.pallas_call(
        functools.partial(exchange_kernel, count),
        out_shape=jax.ShapeDtypeStruct(x.shape, x.dtype),
        in_specs=[pl.BlockSpec(memory_space=pl.ANY)],
        out_specs=pl.BlockSpec(memory_space=pl.ANY),
        scratch_shapes=[
            pltpu.SemaphoreType.DMA((count,)),
            pltpu.SemaphoreType.DMA((count,)),
            pltpu.SemaphoreType.DMA(()),
        ],
        compiler_params=pltpu.CompilerParams(collective_id=tag, has_side_effects=True),
        cost_estimate=pl.CostEstimate(flops=0, transcendentals=0, bytes_accessed=2 * size),
    )(x)


EPSILON = 1e-06


def passed_along(block, axis, distance):
    devices = range(lax.axis_size(axis))
    route = [(i - distance, i) for i in devices if i - distance in devices]
    return lax.ppermute(block, axis, route)


def routing_tables(expert_ids, gate_values, capacity, expert_count):
    row_count, top_count = expert_ids.shape
    flat_ids = expert_ids.reshape(row_count * top_count)
    onehot = (flat_ids[:, None] == jnp.arange(expert_count, dtype=jnp.int32)[None, :]).astype(
        jnp.int32
    )
    earlier = jnp.cumsum(onehot, axis=0) - onehot
    ranks = jnp.sum(earlier * onehot, axis=1)
    slots = flat_ids * capacity + ranks
    hits = (slots[:, None] == jnp.arange(expert_count * capacity, dtype=jnp.int32)[None, :]).astype(
        jnp.float32
    )
    hits = hits.reshape(row_count, top_count, expert_count * capacity)
    picker = jnp.sum(hits, axis=1)
    weigher = jnp.sum(hits * gate_values[:, :, None], axis=1)
    return (picker, weigher)


def replica_sum(per_replica):
    total = jnp.zeros(per_replica.shape[1:], jnp.float32)
    for replica in range(per_replica.shape[0]):
        total = total + lax.optimization_barrier(per_replica[replica].astype(jnp.bfloat16)).astype(
            jnp.float32
        )
    return total


def renew(weights, grads, axis_number, rate):
    scale = jnp.sqrt(jnp.mean(grads * grads, axis=axis_number, keepdims=True) + EPSILON)
    return (weights.astype(jnp.float32) - rate * grads / scale).astype(jnp.bfloat16)


def forward_core(rows_four, weights_gu, weights_dn, part_count):
    ep_count, rep_count, capacity, model_width = rows_four.shape
    hidden_count = weights_gu.shape[2]
    slot_count = ep_count * rep_count * capacity
    both = jnp.dot(
        rows_four.reshape(slot_count, model_width),
        weights_gu.reshape(model_width, 2 * hidden_count),
        preferred_element_type=jnp.float32,
    ).reshape(slot_count, 2, hidden_count)
    active = both[:, 0]
    upward = both[:, 1]
    hidden = (active * jax.nn.sigmoid(active) * upward).astype(jnp.bfloat16)
    piece = jnp.dot(hidden, weights_dn, preferred_element_type=jnp.float32)
    pieces = piece.astype(jnp.bfloat16).reshape(ep_count, rep_count, 1, capacity, model_width)
    return pieces.reshape(ep_count, rep_count * part_count, capacity, model_width)


def learn_core(rows_four, grads_four, weights_gu, weights_dn, part_count):
    ep_count, rep_count, capacity, model_width = rows_four.shape
    hidden_count = weights_gu.shape[2]
    slot_count = ep_count * rep_count * capacity
    flat_grads = grads_four.reshape(slot_count, model_width)
    both = jnp.dot(
        rows_four.reshape(slot_count, model_width),
        weights_gu.reshape(model_width, 2 * hidden_count),
        preferred_element_type=jnp.float32,
    ).reshape(slot_count, 2, hidden_count)
    active = both[:, 0]
    upward = both[:, 1]
    sigma = jax.nn.sigmoid(active)
    swish = active * sigma
    hidden = (swish * upward).astype(jnp.bfloat16)
    back = lax.dot_general(
        flat_grads, weights_dn, (((1,), (1,)), ((), ())), preferred_element_type=jnp.float32
    )
    d_active = back * upward * sigma * (1.0 + active * (1.0 - sigma))
    d_upward = back * swish
    d_both = jnp.stack([d_active, d_upward], axis=1).astype(jnp.bfloat16)
    grad_dn = jnp.einsum(
        "epch,epcd->phd",
        hidden.reshape(ep_count, rep_count, capacity, hidden_count),
        grads_four,
        preferred_element_type=jnp.float32,
    )
    grad_gu = jnp.einsum(
        "epcd,epcgh->pdgh",
        rows_four,
        d_both.reshape(ep_count, rep_count, capacity, 2, hidden_count),
        preferred_element_type=jnp.float32,
    )
    piece = jnp.einsum("mgh,dgh->md", d_both, weights_gu, preferred_element_type=jnp.float32)
    pieces = piece.astype(jnp.bfloat16).reshape(ep_count, rep_count, 1, capacity, model_width)
    ahead = jnp.dot(hidden, weights_dn, preferred_element_type=jnp.float32)
    forward_pieces = ahead.astype(jnp.bfloat16).reshape(
        ep_count, rep_count, 1, capacity, model_width
    )
    slot_dx = pieces.reshape(ep_count, rep_count * part_count, capacity, model_width)
    slot_fw = forward_pieces.reshape(ep_count, rep_count * part_count, capacity, model_width)
    return (grad_gu, grad_dn, slot_dx, slot_fw)


def per_device(
    rows_in,
    cotangent,
    lengths,
    train_experts,
    train_gates,
    decode_experts,
    decode_gates,
    gate_up,
    down,
):
    ep_count = lax.axis_size("ep")
    dp_count = lax.axis_size("dp")
    row_count, model_width = cotangent.shape
    top_count = train_experts.shape[1]
    capacity = min(row_count, max(2, 4 * row_count * top_count // (3 * ep_count)))
    is_learner = lax.axis_index("grp") == 0
    own_gu = gate_up[0, 0]
    own_dn = down[0, 0]
    hidden_all = own_gu.shape[2] * dp_count

    def spread(stacked, tag):
        arrived = jnp.moveaxis(exchange(jnp.moveaxis(stacked, 1, 0), tag), 0, 1)
        return lax.all_gather(arrived, "dp", axis=2)

    def weights_for(weights_gu, weights_dn):
        return (weights_gu, weights_dn, 1)

    def bring_back(slot_out, tag):
        mine = lax.axis_index("dp")
        keep = lax.dynamic_index_in_dim(slot_out, mine, axis=1, keepdims=False)
        give = lax.dynamic_index_in_dim(slot_out, 1 - mine, axis=1, keepdims=False)
        got = lax.ppermute(give, "dp", [(0, 1), (1, 0)])
        summed = (keep.astype(jnp.float32) + got.astype(jnp.float32)).astype(jnp.bfloat16)
        return exchange(summed, tag)

    def combine(mixing, returned):
        total = returned.astype(jnp.float32).reshape(ep_count * capacity, model_width)
        return jnp.einsum("rs,sd->rd", mixing, total, precision=lax.Precision.HIGHEST)

    def dispatch(picker, values):
        buffer = jnp.einsum(
            "rs,rd->sd", picker.astype(jnp.bfloat16), values, preferred_element_type=jnp.float32
        )
        return buffer.astype(jnp.bfloat16)

    tokens = rows_in[0]
    total_rows = row_count * ep_count * dp_count
    longest = 2 * total_rows // lengths.shape[0]
    first_row = (lax.axis_index("ep") * dp_count + lax.axis_index("dp")) * row_count
    places = first_row + jnp.arange(row_count, dtype=jnp.int32)
    ends = jnp.cumsum(lengths)
    starts = ends - lengths
    inside = (places[:, None] >= starts[None, :]) & (places[:, None] < ends[None, :])
    seq_len = jnp.sum(jnp.where(inside, lengths[None, :], 0), axis=1).astype(jnp.float32)
    weight = 2.0 * longest / (seq_len + longest)
    route_ids = jnp.where(is_learner, train_experts, decode_experts[0])
    route_gates = jnp.where(is_learner, train_gates, decode_gates[0])
    picker, weigher = routing_tables(route_ids, route_gates, capacity, ep_count)
    row_buffer = dispatch(picker, tokens)
    cot_wide = cotangent.astype(jnp.float32)
    grad_buffer = jnp.einsum(
        "rs,rd->sd", weigher * weight[:, None], cot_wide, precision=lax.Precision.HIGHEST
    ).astype(jnp.bfloat16)
    stacked = jnp.stack([row_buffer, grad_buffer], axis=0).reshape(
        2, ep_count, capacity, model_width
    )
    arrived = spread(stacked, 0)
    use_gu, use_dn, part_count = weights_for(own_gu, own_dn)
    per_gu, per_dn, slot_dx, slot_fw = learn_core(
        arrived[0], arrived[1], use_gu, use_dn, part_count
    )
    grad_gu = replica_sum(per_gu)
    grad_dn = replica_sum(per_dn)
    returned = bring_back(jnp.where(is_learner, slot_dx, slot_fw), 1)
    mixing = jnp.where(is_learner, picker, weigher)
    base = jnp.where(is_learner, weight[:, None] * cot_wide, tokens.astype(jnp.float32))
    carried = (base + combine(mixing, returned)).astype(jnp.bfloat16)
    sent_gu = renew(own_gu, grad_gu, 0, 0.5 / model_width**0.5)
    sent_dn = renew(own_dn, grad_dn, 1, 0.5 / hidden_all**0.5)
    fresh_gu, fresh_dn = sent_gu, sent_dn
    current = passed_along(carried, "grp", -1)
    picker, weigher = routing_tables(decode_experts[1], decode_gates[1], capacity, ep_count)
    stacked = dispatch(picker, current).reshape(1, ep_count, capacity, model_width)
    arrived = spread(stacked, 2)
    use_gu, use_dn, part_count = weights_for(fresh_gu, fresh_dn)
    slot_out = forward_core(arrived[0], use_gu, use_dn, part_count)
    returned = bring_back(slot_out, 3)
    current = (current.astype(jnp.float32) + combine(weigher, returned)).astype(jnp.bfloat16)
    final_rows = jnp.where(is_learner, carried, passed_along(current, "grp", 1))
    return final_rows[None]


def solution(mesh):
    placed = (
        P("grp", ("ep", "dp"), None),
        P(("ep", "dp"), None),
        P(),
        P(("ep", "dp"), None),
        P(("ep", "dp"), None),
        P(None, ("ep", "dp"), None),
        P(None, ("ep", "dp"), None),
        P("grp", "ep", None, None, "dp"),
        P("grp", "ep", "dp", None),
    )
    return jax.shard_map(
        per_device,
        mesh=mesh,
        in_specs=placed,
        out_specs=P("grp", ("ep", "dp"), None),
        check_vma=False,
    )
```

```python
import jax
import jax.numpy as jnp
from jax import lax
from jax.experimental import pallas as pl
from jax.experimental.pallas import tpu as pltpu
from jax.sharding import PartitionSpec as P
import functools

MESH = pl.DeviceIdType.MESH


def exchange_kernel(count, x_ref, y_ref, send_sem, recv_sem, own_sem):
    me = lax.axis_index("ep")
    barrier = pltpu.get_barrier_semaphore()

    def greet(k, carry):
        other = lax.rem(me + k, count)
        pl.semaphore_signal(barrier, inc=1, device_id={"ep": other}, device_id_type=MESH)
        return carry

    lax.fori_loop(1, count, greet, 0)
    pl.semaphore_wait(barrier, count - 1)
    own = pltpu.make_async_copy(x_ref.at[me], y_ref.at[me], own_sem)
    own.start()

    def outgoing(k):
        other = lax.rem(me + k, count)
        return pltpu.make_async_remote_copy(
            src_ref=x_ref.at[other],
            dst_ref=y_ref.at[me],
            send_sem=send_sem.at[other],
            recv_sem=recv_sem.at[me],
            device_id={"ep": other},
            device_id_type=MESH,
        )

    def incoming(k):
        other = lax.rem(me + count - k, count)
        return pltpu.make_async_remote_copy(
            src_ref=x_ref.at[other],
            dst_ref=y_ref.at[other],
            send_sem=send_sem.at[other],
            recv_sem=recv_sem.at[other],
            device_id={"ep": other},
            device_id_type=MESH,
        )

    def launch(k, carry):
        outgoing(k).start()
        return carry

    lax.fori_loop(1, count, launch, 0)

    def settle(k, carry):
        outgoing(k).wait_send()
        return carry

    lax.fori_loop(1, count, settle, 0)

    def land(k, carry):
        incoming(k).wait_recv()
        return carry

    lax.fori_loop(1, count, land, 0)
    own.wait()


def exchange(x, tag):
    count = x.shape[0]
    size = x.size * x.dtype.itemsize
    return pl.pallas_call(
        functools.partial(exchange_kernel, count),
        out_shape=jax.ShapeDtypeStruct(x.shape, x.dtype),
        in_specs=[pl.BlockSpec(memory_space=pl.ANY)],
        out_specs=pl.BlockSpec(memory_space=pl.ANY),
        scratch_shapes=[
            pltpu.SemaphoreType.DMA((count,)),
            pltpu.SemaphoreType.DMA((count,)),
            pltpu.SemaphoreType.DMA(()),
        ],
        compiler_params=pltpu.CompilerParams(collective_id=tag, has_side_effects=True),
        cost_estimate=pl.CostEstimate(flops=0, transcendentals=0, bytes_accessed=2 * size),
    )(x)


EPSILON = 1e-06


def passed_along(block, axis, distance):
    devices = range(lax.axis_size(axis))
    route = [(i - distance, i) for i in devices if i - distance in devices]
    return lax.ppermute(block, axis, route)


def routing_tables(expert_ids, gate_values, capacity, expert_count):
    row_count, top_count = expert_ids.shape
    flat_ids = expert_ids.reshape(row_count * top_count)
    onehot = (flat_ids[:, None] == jnp.arange(expert_count, dtype=jnp.int32)[None, :]).astype(
        jnp.int32
    )
    earlier = jnp.cumsum(onehot, axis=0) - onehot
    ranks = jnp.sum(earlier * onehot, axis=1)
    slots = flat_ids * capacity + ranks
    hits = (slots[:, None] == jnp.arange(expert_count * capacity, dtype=jnp.int32)[None, :]).astype(
        jnp.float32
    )
    hits = hits.reshape(row_count, top_count, expert_count * capacity)
    picker = jnp.sum(hits, axis=1)
    weigher = jnp.sum(hits * gate_values[:, :, None], axis=1)
    return (picker, weigher)


def replica_sum(per_replica):
    total = jnp.zeros(per_replica.shape[1:], jnp.float32)
    for replica in range(per_replica.shape[0]):
        total = total + lax.optimization_barrier(per_replica[replica].astype(jnp.bfloat16)).astype(
            jnp.float32
        )
    return total


def renew(weights, grads, axis_number, rate):
    scale = jnp.sqrt(jnp.mean(grads * grads, axis=axis_number, keepdims=True) + EPSILON)
    return (weights.astype(jnp.float32) - rate * grads / scale).astype(jnp.bfloat16)


def forward_core(rows_four, weights_gu, weights_dn, part_count):
    ep_count, rep_count, capacity, model_width = rows_four.shape
    hidden_count = weights_gu.shape[2]
    slot_count = ep_count * rep_count * capacity
    both = jnp.dot(
        rows_four.reshape(slot_count, model_width),
        weights_gu.reshape(model_width, 2 * hidden_count),
        preferred_element_type=jnp.float32,
    ).reshape(slot_count, 2, hidden_count)
    active = both[:, 0]
    upward = both[:, 1]
    hidden = (active * jax.nn.sigmoid(active) * upward).astype(jnp.bfloat16)
    piece = jnp.dot(hidden, weights_dn, preferred_element_type=jnp.float32)
    pieces = piece.astype(jnp.bfloat16).reshape(ep_count, rep_count, 1, capacity, model_width)
    return pieces.reshape(ep_count, rep_count * part_count, capacity, model_width)


def learn_core(rows_four, grads_four, weights_gu, weights_dn, part_count):
    ep_count, rep_count, capacity, model_width = rows_four.shape
    hidden_count = weights_gu.shape[2]
    slot_count = ep_count * rep_count * capacity
    flat_grads = grads_four.reshape(slot_count, model_width)
    both = jnp.dot(
        rows_four.reshape(slot_count, model_width),
        weights_gu.reshape(model_width, 2 * hidden_count),
        preferred_element_type=jnp.float32,
    ).reshape(slot_count, 2, hidden_count)
    active = both[:, 0]
    upward = both[:, 1]
    sigma = jax.nn.sigmoid(active)
    swish = active * sigma
    hidden = (swish * upward).astype(jnp.bfloat16)
    back = lax.dot_general(
        flat_grads, weights_dn, (((1,), (1,)), ((), ())), preferred_element_type=jnp.float32
    )
    d_active = back * upward * sigma * (1.0 + active * (1.0 - sigma))
    d_upward = back * swish
    d_both = jnp.stack([d_active, d_upward], axis=1).astype(jnp.bfloat16)
    grad_dn = jnp.einsum(
        "epch,epcd->phd",
        hidden.reshape(ep_count, rep_count, capacity, hidden_count),
        grads_four,
        preferred_element_type=jnp.float32,
    )
    grad_gu = jnp.einsum(
        "epcd,epcgh->pdgh",
        rows_four,
        d_both.reshape(ep_count, rep_count, capacity, 2, hidden_count),
        preferred_element_type=jnp.float32,
    )
    piece = jnp.einsum("mgh,dgh->md", d_both, weights_gu, preferred_element_type=jnp.float32)
    pieces = piece.astype(jnp.bfloat16).reshape(ep_count, rep_count, 1, capacity, model_width)
    ahead = jnp.dot(hidden, weights_dn, preferred_element_type=jnp.float32)
    forward_pieces = ahead.astype(jnp.bfloat16).reshape(
        ep_count, rep_count, 1, capacity, model_width
    )
    slot_dx = pieces.reshape(ep_count, rep_count * part_count, capacity, model_width)
    slot_fw = forward_pieces.reshape(ep_count, rep_count * part_count, capacity, model_width)
    return (grad_gu, grad_dn, slot_dx, slot_fw)


def per_device(
    rows_in,
    cotangent,
    lengths,
    train_experts,
    train_gates,
    decode_experts,
    decode_gates,
    gate_up,
    down,
):
    ep_count = lax.axis_size("ep")
    dp_count = lax.axis_size("dp")
    row_count, model_width = cotangent.shape
    top_count = train_experts.shape[1]
    capacity = min(row_count, max(2, 4 * row_count * top_count // (3 * ep_count)))
    is_learner = lax.axis_index("grp") == 0
    own_gu = gate_up[0, 0]
    own_dn = down[0, 0]
    hidden_all = own_gu.shape[2] * dp_count

    def spread(stacked, tag, native=False):
        if native:
            arrived = lax.all_to_all(stacked, "ep", split_axis=1, concat_axis=1, tiled=True)
        else:
            arrived = jnp.moveaxis(exchange(jnp.moveaxis(stacked, 1, 0), tag), 0, 1)
        return lax.all_gather(arrived, "dp", axis=2)

    def weights_for(weights_gu, weights_dn):
        return (weights_gu, weights_dn, 1)

    def bring_back(slot_out, tag, native=False):
        mine = lax.axis_index("dp")
        keep = lax.dynamic_index_in_dim(slot_out, mine, axis=1, keepdims=False)
        give = lax.dynamic_index_in_dim(slot_out, 1 - mine, axis=1, keepdims=False)
        got = lax.ppermute(give, "dp", [(0, 1), (1, 0)])
        summed = (keep.astype(jnp.float32) + got.astype(jnp.float32)).astype(jnp.bfloat16)
        if native:
            return lax.all_to_all(summed, "ep", split_axis=0, concat_axis=0, tiled=True)
        return exchange(summed, tag)

    def combine(mixing, returned):
        total = returned.astype(jnp.float32).reshape(ep_count * capacity, model_width)
        return jnp.einsum("rs,sd->rd", mixing, total, precision=lax.Precision.HIGHEST)

    def dispatch(picker, values):
        buffer = jnp.einsum(
            "rs,rd->sd", picker.astype(jnp.bfloat16), values, preferred_element_type=jnp.float32
        )
        return buffer.astype(jnp.bfloat16)

    tokens = rows_in[0]
    total_rows = row_count * ep_count * dp_count
    longest = 2 * total_rows // lengths.shape[0]
    first_row = (lax.axis_index("ep") * dp_count + lax.axis_index("dp")) * row_count
    places = first_row + jnp.arange(row_count, dtype=jnp.int32)
    ends = jnp.cumsum(lengths)
    starts = ends - lengths
    inside = (places[:, None] >= starts[None, :]) & (places[:, None] < ends[None, :])
    seq_len = jnp.sum(jnp.where(inside, lengths[None, :], 0), axis=1).astype(jnp.float32)
    weight = 2.0 * longest / (seq_len + longest)
    route_ids = jnp.where(is_learner, train_experts, decode_experts[0])
    route_gates = jnp.where(is_learner, train_gates, decode_gates[0])
    picker, weigher = routing_tables(route_ids, route_gates, capacity, ep_count)
    row_buffer = dispatch(picker, tokens)
    cot_wide = cotangent.astype(jnp.float32)
    grad_buffer = jnp.einsum(
        "rs,rd->sd", weigher * weight[:, None], cot_wide, precision=lax.Precision.HIGHEST
    ).astype(jnp.bfloat16)
    stacked = jnp.stack([row_buffer, grad_buffer], axis=0).reshape(
        2, ep_count, capacity, model_width
    )
    arrived = spread(stacked, 0)
    use_gu, use_dn, part_count = weights_for(own_gu, own_dn)
    per_gu, per_dn, slot_dx, slot_fw = learn_core(
        arrived[0], arrived[1], use_gu, use_dn, part_count
    )
    returned = bring_back(slot_fw, 1, native=True)
    rolled = (tokens.astype(jnp.float32) + combine(weigher, returned)).astype(jnp.bfloat16)
    current = passed_along(rolled, "grp", -1)
    ahead_picker, ahead_weigher = routing_tables(
        decode_experts[1], decode_gates[1], capacity, ep_count
    )
    stacked = dispatch(ahead_picker, current).reshape(1, ep_count, capacity, model_width)
    arrived = spread(stacked, 2, native=True)
    grad_gu = replica_sum(per_gu)
    grad_dn = replica_sum(per_dn)
    fresh_gu = renew(own_gu, grad_gu, 0, 0.5 / model_width**0.5)
    fresh_dn = renew(own_dn, grad_dn, 1, 0.5 / hidden_all**0.5)
    use_gu, use_dn, part_count = weights_for(fresh_gu, fresh_dn)
    slot_out = forward_core(arrived[0], use_gu, use_dn, part_count)
    returned = bring_back(jnp.stack([slot_out, slot_dx], axis=2), 3)
    current = (current.astype(jnp.float32) + combine(ahead_weigher, returned[:, 0])).astype(
        jnp.bfloat16
    )
    carried = (weight[:, None] * cot_wide + combine(picker, returned[:, 1])).astype(jnp.bfloat16)
    final_rows = jnp.where(is_learner, carried, passed_along(current, "grp", 1))
    return final_rows[None]


def solution(mesh):
    placed = (
        P("grp", ("ep", "dp"), None),
        P(("ep", "dp"), None),
        P(),
        P(("ep", "dp"), None),
        P(("ep", "dp"), None),
        P(None, ("ep", "dp"), None),
        P(None, ("ep", "dp"), None),
        P("grp", "ep", None, None, "dp"),
        P("grp", "ep", "dp", None),
    )
    return jax.shard_map(
        per_device,
        mesh=mesh,
        in_specs=placed,
        out_specs=P("grp", ("ep", "dp"), None),
        check_vma=False,
    )
```

```python
import jax
import jax.numpy as jnp
from jax import lax
from jax.experimental import pallas as pl
from jax.experimental.pallas import tpu as pltpu
from jax.sharding import PartitionSpec as P
import functools

MESH = pl.DeviceIdType.MESH


def exchange_kernel(count, width, *refs):
    parts = len(refs) // 2 - 1
    sources, targets = refs[:parts], refs[parts:2 * parts]
    send_sem, recv_sem, own_sem = refs[2 * parts:]
    me = lax.axis_index("ep")
    barrier = pltpu.get_barrier_semaphore()

    def greet(k, carry):
        other = lax.rem(me + k, count)
        pl.semaphore_signal(barrier, inc=1, device_id={"ep": other}, device_id_type=MESH)
        return carry

    lax.fori_loop(1, count, greet, 0)
    pl.semaphore_wait(barrier, count - 1)
    owns = []
    for part in range(parts):
        here = pl.ds(pl.multiple_of(me * width, width), width)
        own = pltpu.make_async_copy(sources[part].at[here], targets[part].at[here], own_sem.at[part])
        own.start()
        owns.append(own)

    def outgoing(part, k):
        other = lax.rem(me + k, count)
        return pltpu.make_async_remote_copy(
            src_ref=sources[part].at[pl.ds(pl.multiple_of(other * width, width), width)],
            dst_ref=targets[part].at[pl.ds(pl.multiple_of(me * width, width), width)],
            send_sem=send_sem.at[part, other],
            recv_sem=recv_sem.at[part, me],
            device_id={"ep": other},
            device_id_type=MESH,
        )

    def incoming(part, k):
        other = lax.rem(me + count - k, count)
        there = pl.ds(pl.multiple_of(other * width, width), width)
        return pltpu.make_async_remote_copy(
            src_ref=sources[part].at[there],
            dst_ref=targets[part].at[there],
            send_sem=send_sem.at[part, other],
            recv_sem=recv_sem.at[part, other],
            device_id={"ep": other},
            device_id_type=MESH,
        )

    def launch(k, carry):
        for part in range(parts):
            outgoing(part, k).start()
        return carry

    lax.fori_loop(1, count, launch, 0)

    def settle(k, carry):
        for part in range(parts):
            outgoing(part, k).wait_send()
        return carry

    lax.fori_loop(1, count, settle, 0)

    def land(k, carry):
        for part in range(parts):
            incoming(part, k).wait_recv()
        return carry

    lax.fori_loop(1, count, land, 0)
    for own in owns:
        own.wait()


def exchange(blocks, count, tag):
    parts = len(blocks)
    width = blocks[0].shape[0] // count
    size = sum(block.size * block.dtype.itemsize for block in blocks)
    return pl.pallas_call(
        functools.partial(exchange_kernel, count, width),
        out_shape=[jax.ShapeDtypeStruct(block.shape, block.dtype) for block in blocks],
        in_specs=[pl.BlockSpec(memory_space=pl.ANY)] * parts,
        out_specs=[pl.BlockSpec(memory_space=pl.ANY)] * parts,
        scratch_shapes=[
            pltpu.SemaphoreType.DMA((parts, count)),
            pltpu.SemaphoreType.DMA((parts, count)),
            pltpu.SemaphoreType.DMA((parts,)),
        ],
        compiler_params=pltpu.CompilerParams(collective_id=tag, has_side_effects=True),
        cost_estimate=pl.CostEstimate(flops=0, transcendentals=0, bytes_accessed=2 * size),
    )(*blocks)


EPSILON = 1e-06


def passed_along(block, axis, distance):
    devices = range(lax.axis_size(axis))
    route = [(i - distance, i) for i in devices if i - distance in devices]
    return lax.ppermute(block, axis, route)


def routing_tables(expert_ids, gate_values, capacity, expert_count):
    row_count, top_count = expert_ids.shape
    flat_ids = expert_ids.reshape(row_count * top_count)
    onehot = (flat_ids[:, None] == jnp.arange(expert_count, dtype=jnp.int32)[None, :]).astype(
        jnp.int32
    )
    earlier = jnp.cumsum(onehot, axis=0) - onehot
    ranks = jnp.sum(earlier * onehot, axis=1)
    slots = flat_ids * capacity + ranks
    hits = (slots[:, None] == jnp.arange(expert_count * capacity, dtype=jnp.int32)[None, :]).astype(
        jnp.float32
    )
    hits = hits.reshape(row_count, top_count, expert_count * capacity)
    picker = jnp.sum(hits, axis=1)
    weigher = jnp.sum(hits * gate_values[:, :, None], axis=1)
    return (picker, weigher)


def replica_sum(per_replica):
    total = jnp.zeros(per_replica.shape[1:], jnp.float32)
    for replica in range(per_replica.shape[0]):
        total = total + lax.optimization_barrier(per_replica[replica].astype(jnp.bfloat16)).astype(
            jnp.float32
        )
    return total


def renew(weights, grads, axis_number, rate):
    scale = jnp.sqrt(jnp.mean(grads * grads, axis=axis_number, keepdims=True) + EPSILON)
    return (weights.astype(jnp.float32) - rate * grads / scale).astype(jnp.bfloat16)


def forward_core(slot_rows, weights_gu, weights_dn):
    hidden_count = weights_gu.shape[2]
    both = jnp.dot(
        slot_rows,
        weights_gu.reshape(slot_rows.shape[1], 2 * hidden_count),
        preferred_element_type=jnp.float32,
    ).reshape(-1, 2, hidden_count)
    active = both[:, 0]
    upward = both[:, 1]
    hidden = (active * jax.nn.sigmoid(active) * upward).astype(jnp.bfloat16)
    return jnp.dot(hidden, weights_dn, preferred_element_type=jnp.float32).astype(jnp.bfloat16)


def learn_core(slot_rows, slot_grads, weights_gu, weights_dn, rep_count):
    slot_count, model_width = slot_rows.shape
    hidden_count = weights_gu.shape[2]
    both = jnp.dot(
        slot_rows,
        weights_gu.reshape(model_width, 2 * hidden_count),
        preferred_element_type=jnp.float32,
    ).reshape(slot_count, 2, hidden_count)
    active = both[:, 0]
    upward = both[:, 1]
    sigma = jax.nn.sigmoid(active)
    swish = active * sigma
    hidden = (swish * upward).astype(jnp.bfloat16)
    back = lax.dot_general(
        slot_grads, weights_dn, (((1,), (1,)), ((), ())), preferred_element_type=jnp.float32
    )
    d_active = back * upward * sigma * (1.0 + active * (1.0 - sigma))
    d_upward = back * swish
    d_both = jnp.stack([d_active, d_upward], axis=1).astype(jnp.bfloat16)
    grad_dn = jnp.einsum(
        "pch,pcd->phd",
        hidden.reshape(rep_count, -1, hidden_count),
        slot_grads.reshape(rep_count, -1, model_width),
        preferred_element_type=jnp.float32,
    )
    grad_gu = jnp.einsum(
        "pcd,pcgh->pdgh",
        slot_rows.reshape(rep_count, -1, model_width),
        d_both.reshape(rep_count, -1, 2, hidden_count),
        preferred_element_type=jnp.float32,
    )
    slot_dx = jnp.einsum("mgh,dgh->md", d_both, weights_gu, preferred_element_type=jnp.float32)
    slot_fw = jnp.dot(hidden, weights_dn, preferred_element_type=jnp.float32)
    return (grad_gu, grad_dn, slot_dx.astype(jnp.bfloat16), slot_fw.astype(jnp.bfloat16))


def per_device(
    rows_in,
    cotangent,
    lengths,
    train_experts,
    train_gates,
    decode_experts,
    decode_gates,
    gate_up,
    down,
):
    ep_count = lax.axis_size("ep")
    dp_count = lax.axis_size("dp")
    row_count, model_width = cotangent.shape
    top_count = train_experts.shape[1]
    capacity = min(row_count, max(2, 4 * row_count * top_count // (3 * ep_count)))
    is_learner = lax.axis_index("grp") == 0
    own_gu = gate_up[0, 0]
    own_dn = down[0, 0]
    hidden_all = own_gu.shape[2] * dp_count

    def spread(buffers, tag):
        arrived = exchange(buffers, ep_count, tag)
        return [lax.all_gather(block, "dp", axis=0, tiled=True) for block in arrived]

    def bring_back(pieces, tag):
        half = pieces.shape[0] // dp_count
        mine = lax.axis_index("dp")
        keep = lax.dynamic_slice_in_dim(pieces, mine * half, half)
        give = lax.dynamic_slice_in_dim(pieces, (1 - mine) * half, half)
        got = lax.ppermute(give, "dp", [(0, 1), (1, 0)])
        summed = (keep.astype(jnp.float32) + got.astype(jnp.float32)).astype(jnp.bfloat16)
        return exchange([summed], ep_count, tag)[0]

    def combine(mixing, returned):
        total = returned.astype(jnp.float32)
        return jnp.einsum("rs,sd->rd", mixing, total, precision=lax.Precision.HIGHEST)

    def dispatch(picker, values):
        buffer = jnp.einsum(
            "rs,rd->sd", picker.astype(jnp.bfloat16), values, preferred_element_type=jnp.float32
        )
        return buffer.astype(jnp.bfloat16)

    tokens = rows_in[0]
    total_rows = row_count * ep_count * dp_count
    longest = 2 * total_rows // lengths.shape[0]
    first_row = (lax.axis_index("ep") * dp_count + lax.axis_index("dp")) * row_count
    places = first_row + jnp.arange(row_count, dtype=jnp.int32)
    ends = jnp.cumsum(lengths)
    starts = ends - lengths
    inside = (places[:, None] >= starts[None, :]) & (places[:, None] < ends[None, :])
    seq_len = jnp.sum(jnp.where(inside, lengths[None, :], 0), axis=1).astype(jnp.float32)
    weight = 2.0 * longest / (seq_len + longest)
    route_ids = jnp.where(is_learner, train_experts, decode_experts[0])
    route_gates = jnp.where(is_learner, train_gates, decode_gates[0])
    picker, weigher = routing_tables(route_ids, route_gates, capacity, ep_count)
    row_buffer = dispatch(picker, tokens)
    cot_wide = cotangent.astype(jnp.float32)
    grad_buffer = jnp.einsum(
        "rs,rd->sd", weigher * weight[:, None], cot_wide, precision=lax.Precision.HIGHEST
    ).astype(jnp.bfloat16)
    rows_got, grads_got = spread([row_buffer, grad_buffer], 0)
    per_gu, per_dn, slot_dx, slot_fw = learn_core(rows_got, grads_got, own_gu, own_dn, dp_count)
    grad_gu = replica_sum(per_gu)
    grad_dn = replica_sum(per_dn)
    returned = bring_back(jnp.where(is_learner, slot_dx, slot_fw), 1)
    mixing = jnp.where(is_learner, picker, weigher)
    base = jnp.where(is_learner, weight[:, None] * cot_wide, tokens.astype(jnp.float32))
    carried = (base + combine(mixing, returned)).astype(jnp.bfloat16)
    fresh_gu = renew(own_gu, grad_gu, 0, 0.5 / model_width**0.5)
    fresh_dn = renew(own_dn, grad_dn, 1, 0.5 / hidden_all**0.5)
    current = passed_along(carried, "grp", -1)
    picker, weigher = routing_tables(decode_experts[1], decode_gates[1], capacity, ep_count)
    (rows_got,) = spread([dispatch(picker, current)], 2)
    slot_out = forward_core(rows_got, fresh_gu, fresh_dn)
    returned = bring_back(slot_out, 3)
    current = (current.astype(jnp.float32) + combine(weigher, returned)).astype(jnp.bfloat16)
    final_rows = jnp.where(is_learner, carried, passed_along(current, "grp", 1))
    return final_rows[None]


def solution(mesh):
    placed = (
        P("grp", ("ep", "dp"), None),
        P(("ep", "dp"), None),
        P(),
        P(("ep", "dp"), None),
        P(("ep", "dp"), None),
        P(None, ("ep", "dp"), None),
        P(None, ("ep", "dp"), None),
        P("grp", "ep", None, None, "dp"),
        P("grp", "ep", "dp", None),
    )
    return jax.shard_map(
        per_device,
        mesh=mesh,
        in_specs=placed,
        out_specs=P("grp", ("ep", "dp"), None),
        check_vma=False,
    )
```

```python
import jax
import jax.numpy as jnp
from jax import lax
from jax.experimental import pallas as pl
from jax.experimental.pallas import tpu as pltpu
from jax.sharding import PartitionSpec as P
import functools

MESH = pl.DeviceIdType.MESH


def exchange_kernel(count, width, share, *refs):
    parts = len(refs) // 2 - 1
    sources, targets = refs[:parts], refs[parts:2 * parts]
    send_sem, recv_sem, own_sem = refs[2 * parts:]
    me = lax.axis_index("ep")
    rows = count * width
    side = lax.axis_index("dp")
    base = side * rows if share else 0
    barrier = pltpu.get_barrier_semaphore()

    def greet(k, carry):
        other = lax.rem(me + k, count)
        pl.semaphore_signal(barrier, inc=1, device_id={"ep": other}, device_id_type=MESH)
        return carry

    lax.fori_loop(1, count, greet, 0)
    if share:
        pl.semaphore_signal(barrier, inc=1, device_id={"dp": 1 - side}, device_id_type=MESH)
    pl.semaphore_wait(barrier, count - 1 + (1 if share else 0))

    def spot(index, start=0):
        return pl.ds(pl.multiple_of(start + index * width, width), width)

    owns = []
    for part in range(parts):
        own = pltpu.make_async_copy(
            sources[part].at[spot(me)], targets[part].at[spot(me, base)], own_sem.at[part, 0]
        )
        own.start()
        owns.append(own)

    def outgoing(part, k):
        other = lax.rem(me + k, count)
        return pltpu.make_async_remote_copy(
            src_ref=sources[part].at[spot(other)],
            dst_ref=targets[part].at[spot(me, base)],
            send_sem=send_sem.at[part, other],
            recv_sem=recv_sem.at[part, me],
            device_id={"ep": other},
            device_id_type=MESH,
        )

    def incoming(part, k):
        other = lax.rem(me + count - k, count)
        return pltpu.make_async_remote_copy(
            src_ref=sources[part].at[spot(other)],
            dst_ref=targets[part].at[spot(other, base)],
            send_sem=send_sem.at[part, other],
            recv_sem=recv_sem.at[part, other],
            device_id={"ep": other},
            device_id_type=MESH,
        )

    def launch(k, carry):
        for part in range(parts):
            outgoing(part, k).start()
        return carry

    lax.fori_loop(1, count, launch, 0)

    def settle(k, carry):
        for part in range(parts):
            outgoing(part, k).wait_send()
        return carry

    lax.fori_loop(1, count, settle, 0)

    def land(k, carry):
        for part in range(parts):
            incoming(part, k).wait_recv()
        return carry

    lax.fori_loop(1, count, land, 0)
    for own in owns:
        own.wait()
    if share:
        half = pl.ds(pl.multiple_of(base, rows), rows)
        yonder = pl.ds(pl.multiple_of((1 - side) * rows, rows), rows)
        passes = []
        for part in range(parts):
            onward = pltpu.make_async_remote_copy(
                src_ref=targets[part].at[half],
                dst_ref=targets[part].at[half],
                send_sem=own_sem.at[part, 1],
                recv_sem=own_sem.at[part, 2],
                device_id={"dp": 1 - side},
                device_id_type=MESH,
            )
            onward.start()
            passes.append(onward)
        for part in range(parts):
            passes[part].wait_send()
            pltpu.make_async_remote_copy(
                src_ref=targets[part].at[yonder],
                dst_ref=targets[part].at[yonder],
                send_sem=own_sem.at[part, 1],
                recv_sem=own_sem.at[part, 2],
                device_id={"dp": 1 - side},
                device_id_type=MESH,
            ).wait_recv()


def exchange(blocks, count, tag, share=False):
    parts = len(blocks)
    width = blocks[0].shape[0] // count
    grow = 2 if share else 1
    size = sum(block.size * block.dtype.itemsize for block in blocks)
    return pl.pallas_call(
        functools.partial(exchange_kernel, count, width, share),
        out_shape=[
            jax.ShapeDtypeStruct((grow * block.shape[0],) + block.shape[1:], block.dtype)
            for block in blocks
        ],
        in_specs=[pl.BlockSpec(memory_space=pl.ANY)] * parts,
        out_specs=[pl.BlockSpec(memory_space=pl.ANY)] * parts,
        scratch_shapes=[
            pltpu.SemaphoreType.DMA((parts, count)),
            pltpu.SemaphoreType.DMA((parts, count)),
            pltpu.SemaphoreType.DMA((parts, 3)),
        ],
        compiler_params=pltpu.CompilerParams(collective_id=tag, has_side_effects=True),
        cost_estimate=pl.CostEstimate(
            flops=0, transcendentals=0, bytes_accessed=(2 + 2 * grow) * size
        ),
    )(*blocks)


EPSILON = 1e-06


def passed_along(block, axis, distance):
    devices = range(lax.axis_size(axis))
    route = [(i - distance, i) for i in devices if i - distance in devices]
    return lax.ppermute(block, axis, route)


def routing_tables(expert_ids, gate_values, capacity, expert_count):
    row_count, top_count = expert_ids.shape
    flat_ids = expert_ids.reshape(row_count * top_count)
    onehot = (flat_ids[:, None] == jnp.arange(expert_count, dtype=jnp.int32)[None, :]).astype(
        jnp.int32
    )
    earlier = jnp.cumsum(onehot, axis=0) - onehot
    ranks = jnp.sum(earlier * onehot, axis=1)
    slots = flat_ids * capacity + ranks
    hits = (slots[:, None] == jnp.arange(expert_count * capacity, dtype=jnp.int32)[None, :]).astype(
        jnp.float32
    )
    hits = hits.reshape(row_count, top_count, expert_count * capacity)
    picker = jnp.sum(hits, axis=1)
    weigher = jnp.sum(hits * gate_values[:, :, None], axis=1)
    return (picker, weigher)


def replica_sum(per_replica):
    total = jnp.zeros(per_replica.shape[1:], jnp.float32)
    for replica in range(per_replica.shape[0]):
        total = total + lax.optimization_barrier(per_replica[replica].astype(jnp.bfloat16)).astype(
            jnp.float32
        )
    return total


def renew(weights, grads, axis_number, rate):
    scale = jnp.sqrt(jnp.mean(grads * grads, axis=axis_number, keepdims=True) + EPSILON)
    return (weights.astype(jnp.float32) - rate * grads / scale).astype(jnp.bfloat16)


def forward_core(slot_rows, weights_gu, weights_dn):
    hidden_count = weights_gu.shape[2]
    both = jnp.dot(
        slot_rows,
        weights_gu.reshape(slot_rows.shape[1], 2 * hidden_count),
        preferred_element_type=jnp.float32,
    ).reshape(-1, 2, hidden_count)
    active = both[:, 0]
    upward = both[:, 1]
    hidden = (active * jax.nn.sigmoid(active) * upward).astype(jnp.bfloat16)
    return jnp.dot(hidden, weights_dn, preferred_element_type=jnp.float32).astype(jnp.bfloat16)


def learn_core(slot_rows, slot_grads, weights_gu, weights_dn, rep_count):
    slot_count, model_width = slot_rows.shape
    hidden_count = weights_gu.shape[2]
    both = jnp.dot(
        slot_rows,
        weights_gu.reshape(model_width, 2 * hidden_count),
        preferred_element_type=jnp.float32,
    ).reshape(slot_count, 2, hidden_count)
    active = both[:, 0]
    upward = both[:, 1]
    sigma = jax.nn.sigmoid(active)
    swish = active * sigma
    hidden = (swish * upward).astype(jnp.bfloat16)
    back = lax.dot_general(
        slot_grads, weights_dn, (((1,), (1,)), ((), ())), preferred_element_type=jnp.float32
    )
    d_active = back * upward * sigma * (1.0 + active * (1.0 - sigma))
    d_upward = back * swish
    d_both = jnp.stack([d_active, d_upward], axis=1).astype(jnp.bfloat16)
    grad_dn = jnp.einsum(
        "pch,pcd->phd",
        hidden.reshape(rep_count, -1, hidden_count),
        slot_grads.reshape(rep_count, -1, model_width),
        preferred_element_type=jnp.float32,
    )
    grad_gu = jnp.einsum(
        "pcd,pcgh->pdgh",
        slot_rows.reshape(rep_count, -1, model_width),
        d_both.reshape(rep_count, -1, 2, hidden_count),
        preferred_element_type=jnp.float32,
    )
    slot_dx = jnp.einsum("mgh,dgh->md", d_both, weights_gu, preferred_element_type=jnp.float32)
    slot_fw = jnp.dot(hidden, weights_dn, preferred_element_type=jnp.float32)
    return (grad_gu, grad_dn, slot_dx.astype(jnp.bfloat16), slot_fw.astype(jnp.bfloat16))


def per_device(
    rows_in,
    cotangent,
    lengths,
    train_experts,
    train_gates,
    decode_experts,
    decode_gates,
    gate_up,
    down,
):
    ep_count = lax.axis_size("ep")
    dp_count = lax.axis_size("dp")
    row_count, model_width = cotangent.shape
    top_count = train_experts.shape[1]
    capacity = min(row_count, max(2, 4 * row_count * top_count // (3 * ep_count)))
    is_learner = lax.axis_index("grp") == 0
    own_gu = gate_up[0, 0]
    own_dn = down[0, 0]
    hidden_all = own_gu.shape[2] * dp_count

    def spread(buffers, tag):
        return exchange(buffers, ep_count, tag, share=True)

    def bring_back(pieces, tag):
        half = pieces.shape[0] // dp_count
        mine = lax.axis_index("dp")
        keep = lax.dynamic_slice_in_dim(pieces, mine * half, half)
        give = lax.dynamic_slice_in_dim(pieces, (1 - mine) * half, half)
        got = lax.ppermute(give, "dp", [(0, 1), (1, 0)])
        summed = (keep.astype(jnp.float32) + got.astype(jnp.float32)).astype(jnp.bfloat16)
        return exchange([summed], ep_count, tag)[0]

    def combine(mixing, returned):
        total = returned.astype(jnp.float32)
        return jnp.einsum("rs,sd->rd", mixing, total, precision=lax.Precision.HIGHEST)

    def dispatch(picker, values):
        buffer = jnp.einsum(
            "rs,rd->sd", picker.astype(jnp.bfloat16), values, preferred_element_type=jnp.float32
        )
        return buffer.astype(jnp.bfloat16)

    tokens = rows_in[0]
    total_rows = row_count * ep_count * dp_count
    longest = 2 * total_rows // lengths.shape[0]
    first_row = (lax.axis_index("ep") * dp_count + lax.axis_index("dp")) * row_count
    places = first_row + jnp.arange(row_count, dtype=jnp.int32)
    ends = jnp.cumsum(lengths)
    starts = ends - lengths
    inside = (places[:, None] >= starts[None, :]) & (places[:, None] < ends[None, :])
    seq_len = jnp.sum(jnp.where(inside, lengths[None, :], 0), axis=1).astype(jnp.float32)
    weight = 2.0 * longest / (seq_len + longest)
    route_ids = jnp.where(is_learner, train_experts, decode_experts[0])
    route_gates = jnp.where(is_learner, train_gates, decode_gates[0])
    picker, weigher = routing_tables(route_ids, route_gates, capacity, ep_count)
    row_buffer = dispatch(picker, tokens)
    cot_wide = cotangent.astype(jnp.float32)
    grad_buffer = jnp.einsum(
        "rs,rd->sd", weigher * weight[:, None], cot_wide, precision=lax.Precision.HIGHEST
    ).astype(jnp.bfloat16)
    rows_got, grads_got = spread([row_buffer, grad_buffer], 0)
    per_gu, per_dn, slot_dx, slot_fw = learn_core(rows_got, grads_got, own_gu, own_dn, dp_count)
    grad_gu = replica_sum(per_gu)
    grad_dn = replica_sum(per_dn)
    returned = bring_back(jnp.where(is_learner, slot_dx, slot_fw), 1)
    mixing = jnp.where(is_learner, picker, weigher)
    base = jnp.where(is_learner, weight[:, None] * cot_wide, tokens.astype(jnp.float32))
    carried = (base + combine(mixing, returned)).astype(jnp.bfloat16)
    fresh_gu = renew(own_gu, grad_gu, 0, 0.5 / model_width**0.5)
    fresh_dn = renew(own_dn, grad_dn, 1, 0.5 / hidden_all**0.5)
    current = passed_along(carried, "grp", -1)
    picker, weigher = routing_tables(decode_experts[1], decode_gates[1], capacity, ep_count)
    (rows_got,) = spread([dispatch(picker, current)], 2)
    slot_out = forward_core(rows_got, fresh_gu, fresh_dn)
    returned = bring_back(slot_out, 3)
    current = (current.astype(jnp.float32) + combine(weigher, returned)).astype(jnp.bfloat16)
    final_rows = jnp.where(is_learner, carried, passed_along(current, "grp", 1))
    return final_rows[None]


def solution(mesh):
    placed = (
        P("grp", ("ep", "dp"), None),
        P(("ep", "dp"), None),
        P(),
        P(("ep", "dp"), None),
        P(("ep", "dp"), None),
        P(None, ("ep", "dp"), None),
        P(None, ("ep", "dp"), None),
        P("grp", "ep", None, None, "dp"),
        P("grp", "ep", "dp", None),
    )
    return jax.shard_map(
        per_device,
        mesh=mesh,
        in_specs=placed,
        out_specs=P("grp", ("ep", "dp"), None),
        check_vma=False,
    )
```

```python
import jax
import jax.numpy as jnp
from jax import lax
from jax.experimental import pallas as pl
from jax.experimental.pallas import tpu as pltpu
from jax.sharding import PartitionSpec as P
import functools

MESH = pl.DeviceIdType.MESH


def exchange_kernel(count, width, share, *refs):
    parts = len(refs) // 2 - 1
    sources, targets = refs[:parts], refs[parts:2 * parts]
    send_sem, recv_sem, own_sem = refs[2 * parts:]
    me = lax.axis_index("ep")
    rows = count * width
    side = lax.axis_index("dp")
    base = side * rows if share else 0
    barrier = pltpu.get_barrier_semaphore()

    def greet(k, carry):
        other = lax.rem(me + k, count)
        pl.semaphore_signal(barrier, inc=1, device_id={"ep": other}, device_id_type=MESH)
        return carry

    lax.fori_loop(1, count, greet, 0)
    if share:
        pl.semaphore_signal(barrier, inc=1, device_id={"dp": 1 - side}, device_id_type=MESH)
    pl.semaphore_wait(barrier, count - 1 + (1 if share else 0))

    def spot(index, start=0):
        return pl.ds(pl.multiple_of(start + index * width, width), width)

    owns = []
    for part in range(parts):
        own = pltpu.make_async_copy(
            sources[part].at[spot(me)], targets[part].at[spot(me, base)], own_sem.at[part, 0]
        )
        own.start()
        owns.append(own)

    def outgoing(part, k):
        other = lax.rem(me + k, count)
        return pltpu.make_async_remote_copy(
            src_ref=sources[part].at[spot(other)],
            dst_ref=targets[part].at[spot(me, base)],
            send_sem=send_sem.at[part, other],
            recv_sem=recv_sem.at[part, me],
            device_id={"ep": other},
            device_id_type=MESH,
        )

    def incoming(part, k):
        other = lax.rem(me + count - k, count)
        return pltpu.make_async_remote_copy(
            src_ref=sources[part].at[spot(other)],
            dst_ref=targets[part].at[spot(other, base)],
            send_sem=send_sem.at[part, other],
            recv_sem=recv_sem.at[part, other],
            device_id={"ep": other},
            device_id_type=MESH,
        )

    def launch(k, carry):
        for part in range(parts):
            outgoing(part, k).start()
        return carry

    lax.fori_loop(1, count, launch, 0)

    def settle(k, carry):
        for part in range(parts):
            outgoing(part, k).wait_send()
        return carry

    lax.fori_loop(1, count, settle, 0)

    def land(k, carry):
        for part in range(parts):
            incoming(part, k).wait_recv()
        return carry

    lax.fori_loop(1, count, land, 0)
    for own in owns:
        own.wait()
    if share:
        half = pl.ds(pl.multiple_of(base, rows), rows)
        yonder = pl.ds(pl.multiple_of((1 - side) * rows, rows), rows)
        passes = []
        for part in range(parts):
            onward = pltpu.make_async_remote_copy(
                src_ref=targets[part].at[half],
                dst_ref=targets[part].at[half],
                send_sem=own_sem.at[part, 1],
                recv_sem=own_sem.at[part, 2],
                device_id={"dp": 1 - side},
                device_id_type=MESH,
            )
            onward.start()
            passes.append(onward)
        for part in range(parts):
            passes[part].wait_send()
            pltpu.make_async_remote_copy(
                src_ref=targets[part].at[yonder],
                dst_ref=targets[part].at[yonder],
                send_sem=own_sem.at[part, 1],
                recv_sem=own_sem.at[part, 2],
                device_id={"dp": 1 - side},
                device_id_type=MESH,
            ).wait_recv()


def exchange(blocks, count, tag, share=False):
    parts = len(blocks)
    width = blocks[0].shape[0] // count
    grow = 2 if share else 1
    size = sum(block.size * block.dtype.itemsize for block in blocks)
    return pl.pallas_call(
        functools.partial(exchange_kernel, count, width, share),
        out_shape=[
            jax.ShapeDtypeStruct((grow * block.shape[0],) + block.shape[1:], block.dtype)
            for block in blocks
        ],
        in_specs=[pl.BlockSpec(memory_space=pl.ANY)] * parts,
        out_specs=[pl.BlockSpec(memory_space=pl.ANY)] * parts,
        scratch_shapes=[
            pltpu.SemaphoreType.DMA((parts, count)),
            pltpu.SemaphoreType.DMA((parts, count)),
            pltpu.SemaphoreType.DMA((parts, 3)),
        ],
        compiler_params=pltpu.CompilerParams(collective_id=tag, has_side_effects=True),
        cost_estimate=pl.CostEstimate(
            flops=0, transcendentals=0, bytes_accessed=(2 + 2 * grow) * size
        ),
    )(*blocks)


EPSILON = 1e-06


def passed_along(block, axis, distance):
    devices = range(lax.axis_size(axis))
    route = [(i - distance, i) for i in devices if i - distance in devices]
    return lax.ppermute(block, axis, route)


def routing_tables(expert_ids, gate_values, capacity, expert_count):
    row_count, top_count = expert_ids.shape
    flat_ids = expert_ids.reshape(row_count * top_count)
    onehot = (flat_ids[:, None] == jnp.arange(expert_count, dtype=jnp.int32)[None, :]).astype(
        jnp.int32
    )
    earlier = jnp.cumsum(onehot, axis=0) - onehot
    ranks = jnp.sum(earlier * onehot, axis=1)
    slots = flat_ids * capacity + ranks
    hits = (slots[:, None] == jnp.arange(expert_count * capacity, dtype=jnp.int32)[None, :]).astype(
        jnp.float32
    )
    hits = hits.reshape(row_count, top_count, expert_count * capacity)
    picker = jnp.sum(hits, axis=1)
    weigher = jnp.sum(hits * gate_values[:, :, None], axis=1)
    return (picker, weigher)


def replica_sum(per_replica):
    total = jnp.zeros(per_replica.shape[1:], jnp.float32)
    for replica in range(per_replica.shape[0]):
        total = total + lax.optimization_barrier(per_replica[replica].astype(jnp.bfloat16)).astype(
            jnp.float32
        )
    return total


def renew(weights, grads, axis_number, rate):
    scale = jnp.sqrt(jnp.mean(grads * grads, axis=axis_number, keepdims=True) + EPSILON)
    return (weights.astype(jnp.float32) - rate * grads / scale).astype(jnp.bfloat16)


def forward_core(slot_rows, weights_gu, weights_dn):
    hidden_count = weights_gu.shape[0] // 2
    both = lax.dot_general(
        slot_rows, weights_gu, (((1,), (1,)), ((), ())), preferred_element_type=jnp.float32
    ).reshape(-1, 2, hidden_count)
    active = both[:, 0]
    upward = both[:, 1]
    hidden = (active * jax.nn.sigmoid(active) * upward).astype(jnp.bfloat16)
    return jnp.dot(hidden, weights_dn, preferred_element_type=jnp.float32).astype(jnp.bfloat16)


def learn_core(slot_rows, slot_grads, weights_gu, weights_dn, rep_count):
    slot_count, model_width = slot_rows.shape
    hidden_count = weights_gu.shape[0] // 2
    both = lax.dot_general(
        slot_rows, weights_gu, (((1,), (1,)), ((), ())), preferred_element_type=jnp.float32
    ).reshape(slot_count, 2, hidden_count)
    active = both[:, 0]
    upward = both[:, 1]
    sigma = jax.nn.sigmoid(active)
    swish = active * sigma
    hidden = (swish * upward).astype(jnp.bfloat16)
    back = lax.dot_general(
        slot_grads, weights_dn, (((1,), (1,)), ((), ())), preferred_element_type=jnp.float32
    )
    d_active = back * upward * sigma * (1.0 + active * (1.0 - sigma))
    d_upward = back * swish
    d_both = jnp.stack([d_active, d_upward], axis=1).astype(jnp.bfloat16)
    grad_dn = jnp.einsum(
        "pch,pcd->phd",
        hidden.reshape(rep_count, -1, hidden_count),
        slot_grads.reshape(rep_count, -1, model_width),
        preferred_element_type=jnp.float32,
    )
    grad_gu = jnp.einsum(
        "pcj,pcd->pjd",
        d_both.reshape(rep_count, -1, 2 * hidden_count),
        slot_rows.reshape(rep_count, -1, model_width),
        preferred_element_type=jnp.float32,
    )
    slot_dx = jnp.dot(
        d_both.reshape(slot_count, 2 * hidden_count), weights_gu, preferred_element_type=jnp.float32
    )
    slot_fw = jnp.dot(hidden, weights_dn, preferred_element_type=jnp.float32)
    return (grad_gu, grad_dn, slot_dx.astype(jnp.bfloat16), slot_fw.astype(jnp.bfloat16))


def per_device(
    rows_in,
    cotangent,
    lengths,
    train_experts,
    train_gates,
    decode_experts,
    decode_gates,
    gate_up,
    down,
):
    ep_count = lax.axis_size("ep")
    dp_count = lax.axis_size("dp")
    row_count, model_width = cotangent.shape
    top_count = train_experts.shape[1]
    capacity = min(row_count, max(2, 4 * row_count * top_count // (3 * ep_count)))
    is_learner = lax.axis_index("grp") == 0
    own_gu = gate_up[0, 0].reshape(gate_up.shape[2], -1).T
    own_dn = down[0, 0]
    hidden_all = own_dn.shape[0] * dp_count

    def spread(buffers, tag):
        return exchange(buffers, ep_count, tag, share=True)

    def bring_back(pieces, tag):
        half = pieces.shape[0] // dp_count
        mine = lax.axis_index("dp")
        keep = lax.dynamic_slice_in_dim(pieces, mine * half, half)
        give = lax.dynamic_slice_in_dim(pieces, (1 - mine) * half, half)
        got = lax.ppermute(give, "dp", [(0, 1), (1, 0)])
        summed = (keep.astype(jnp.float32) + got.astype(jnp.float32)).astype(jnp.bfloat16)
        return exchange([summed], ep_count, tag)[0]

    def combine(mixing, returned):
        total = returned.astype(jnp.float32)
        return jnp.einsum("rs,sd->rd", mixing, total, precision=lax.Precision.HIGHEST)

    def dispatch(picker, values):
        buffer = jnp.einsum(
            "rs,rd->sd", picker.astype(jnp.bfloat16), values, preferred_element_type=jnp.float32
        )
        return buffer.astype(jnp.bfloat16)

    tokens = rows_in[0]
    total_rows = row_count * ep_count * dp_count
    longest = 2 * total_rows // lengths.shape[0]
    first_row = (lax.axis_index("ep") * dp_count + lax.axis_index("dp")) * row_count
    places = first_row + jnp.arange(row_count, dtype=jnp.int32)
    ends = jnp.cumsum(lengths)
    starts = ends - lengths
    inside = (places[:, None] >= starts[None, :]) & (places[:, None] < ends[None, :])
    seq_len = jnp.sum(jnp.where(inside, lengths[None, :], 0), axis=1).astype(jnp.float32)
    weight = 2.0 * longest / (seq_len + longest)
    route_ids = jnp.where(is_learner, train_experts, decode_experts[0])
    route_gates = jnp.where(is_learner, train_gates, decode_gates[0])
    picker, weigher = routing_tables(route_ids, route_gates, capacity, ep_count)
    row_buffer = dispatch(picker, tokens)
    cot_wide = cotangent.astype(jnp.float32)
    grad_buffer = jnp.einsum(
        "rs,rd->sd", weigher * weight[:, None], cot_wide, precision=lax.Precision.HIGHEST
    ).astype(jnp.bfloat16)
    rows_got, grads_got = spread([row_buffer, grad_buffer], 0)
    per_gu, per_dn, slot_dx, slot_fw = learn_core(rows_got, grads_got, own_gu, own_dn, dp_count)
    grad_gu = replica_sum(per_gu)
    grad_dn = replica_sum(per_dn)
    returned = bring_back(jnp.where(is_learner, slot_dx, slot_fw), 1)
    mixing = jnp.where(is_learner, picker, weigher)
    base = jnp.where(is_learner, weight[:, None] * cot_wide, tokens.astype(jnp.float32))
    carried = (base + combine(mixing, returned)).astype(jnp.bfloat16)
    fresh_gu = renew(own_gu, grad_gu, 1, 0.5 / model_width**0.5)
    fresh_dn = renew(own_dn, grad_dn, 1, 0.5 / hidden_all**0.5)
    current = passed_along(carried, "grp", -1)
    picker, weigher = routing_tables(decode_experts[1], decode_gates[1], capacity, ep_count)
    (rows_got,) = spread([dispatch(picker, current)], 2)
    slot_out = forward_core(rows_got, fresh_gu, fresh_dn)
    returned = bring_back(slot_out, 3)
    current = (current.astype(jnp.float32) + combine(weigher, returned)).astype(jnp.bfloat16)
    final_rows = jnp.where(is_learner, carried, passed_along(current, "grp", 1))
    return final_rows[None]


def solution(mesh):
    placed = (
        P("grp", ("ep", "dp"), None),
        P(("ep", "dp"), None),
        P(),
        P(("ep", "dp"), None),
        P(("ep", "dp"), None),
        P(None, ("ep", "dp"), None),
        P(None, ("ep", "dp"), None),
        P("grp", "ep", None, None, "dp"),
        P("grp", "ep", "dp", None),
    )
    return jax.shard_map(
        per_device,
        mesh=mesh,
        in_specs=placed,
        out_specs=P("grp", ("ep", "dp"), None),
        check_vma=False,
    )
```

```python
import jax
import jax.numpy as jnp
from jax import lax
from jax.experimental import pallas as pl
from jax.experimental.pallas import tpu as pltpu
from jax.sharding import PartitionSpec as P
import functools

MESH = pl.DeviceIdType.MESH


def exchange_kernel(count, width, share, *refs):
    parts = len(refs) // 2 - 1
    sources, targets = refs[:parts], refs[parts:2 * parts]
    send_sem, recv_sem, own_sem = refs[2 * parts:]
    me = lax.axis_index("ep")
    rows = count * width
    side = lax.axis_index("dp")
    base = side * rows if share else 0
    barrier = pltpu.get_barrier_semaphore()

    def greet(k, carry):
        other = lax.rem(me + k, count)
        pl.semaphore_signal(barrier, inc=1, device_id={"ep": other}, device_id_type=MESH)
        return carry

    lax.fori_loop(1, count, greet, 0)
    if share:
        pl.semaphore_signal(barrier, inc=1, device_id={"dp": 1 - side}, device_id_type=MESH)
    pl.semaphore_wait(barrier, count - 1 + (1 if share else 0))

    def spot(index, start=0):
        return pl.ds(pl.multiple_of(start + index * width, width), width)

    owns = []
    for part in range(parts):
        own = pltpu.make_async_copy(
            sources[part].at[spot(me)], targets[part].at[spot(me, base)], own_sem.at[part, 0]
        )
        own.start()
        owns.append(own)

    def outgoing(part, k):
        step = jnp.where(k % 2 == 1, (k + 1) // 2, count - k // 2)
        other = lax.rem(me + step, count)
        return pltpu.make_async_remote_copy(
            src_ref=sources[part].at[spot(other)],
            dst_ref=targets[part].at[spot(me, base)],
            send_sem=send_sem.at[part, other],
            recv_sem=recv_sem.at[part, me],
            device_id={"ep": other},
            device_id_type=MESH,
        )

    def incoming(part, k):
        other = lax.rem(me + count - k, count)
        return pltpu.make_async_remote_copy(
            src_ref=sources[part].at[spot(other)],
            dst_ref=targets[part].at[spot(other, base)],
            send_sem=send_sem.at[part, other],
            recv_sem=recv_sem.at[part, other],
            device_id={"ep": other},
            device_id_type=MESH,
        )

    def launch(k, carry):
        for part in range(parts):
            outgoing(part, k).start()
        return carry

    lax.fori_loop(1, count, launch, 0)

    def settle(k, carry):
        for part in range(parts):
            outgoing(part, k).wait_send()
        return carry

    lax.fori_loop(1, count, settle, 0)

    def land(k, carry):
        for part in range(parts):
            incoming(part, k).wait_recv()
        return carry

    lax.fori_loop(1, count, land, 0)
    for own in owns:
        own.wait()
    if share:
        half = pl.ds(pl.multiple_of(base, rows), rows)
        yonder = pl.ds(pl.multiple_of((1 - side) * rows, rows), rows)
        passes = []
        for part in range(parts):
            onward = pltpu.make_async_remote_copy(
                src_ref=targets[part].at[half],
                dst_ref=targets[part].at[half],
                send_sem=own_sem.at[part, 1],
                recv_sem=own_sem.at[part, 2],
                device_id={"dp": 1 - side},
                device_id_type=MESH,
            )
            onward.start()
            passes.append(onward)
        for part in range(parts):
            passes[part].wait_send()
            pltpu.make_async_remote_copy(
                src_ref=targets[part].at[yonder],
                dst_ref=targets[part].at[yonder],
                send_sem=own_sem.at[part, 1],
                recv_sem=own_sem.at[part, 2],
                device_id={"dp": 1 - side},
                device_id_type=MESH,
            ).wait_recv()


def exchange(blocks, count, tag, share=False):
    parts = len(blocks)
    width = blocks[0].shape[0] // count
    grow = 2 if share else 1
    size = sum(block.size * block.dtype.itemsize for block in blocks)
    return pl.pallas_call(
        functools.partial(exchange_kernel, count, width, share),
        out_shape=[
            jax.ShapeDtypeStruct((grow * block.shape[0],) + block.shape[1:], block.dtype)
            for block in blocks
        ],
        in_specs=[pl.BlockSpec(memory_space=pl.ANY)] * parts,
        out_specs=[pl.BlockSpec(memory_space=pl.ANY)] * parts,
        scratch_shapes=[
            pltpu.SemaphoreType.DMA((parts, count)),
            pltpu.SemaphoreType.DMA((parts, count)),
            pltpu.SemaphoreType.DMA((parts, 3)),
        ],
        compiler_params=pltpu.CompilerParams(collective_id=tag, has_side_effects=True),
        cost_estimate=pl.CostEstimate(
            flops=0, transcendentals=0, bytes_accessed=(2 + 2 * grow) * size
        ),
    )(*blocks)


EPSILON = 1e-06


def passed_along(block, axis, distance):
    devices = range(lax.axis_size(axis))
    route = [(i - distance, i) for i in devices if i - distance in devices]
    return lax.ppermute(block, axis, route)


def routing_tables(expert_ids, gate_values, capacity, expert_count):
    row_count, top_count = expert_ids.shape
    flat_ids = expert_ids.reshape(row_count * top_count)
    onehot = (flat_ids[:, None] == jnp.arange(expert_count, dtype=jnp.int32)[None, :]).astype(
        jnp.int32
    )
    earlier = jnp.cumsum(onehot, axis=0) - onehot
    ranks = jnp.sum(earlier * onehot, axis=1)
    slots = flat_ids * capacity + ranks
    hits = (slots[:, None] == jnp.arange(expert_count * capacity, dtype=jnp.int32)[None, :]).astype(
        jnp.float32
    )
    hits = hits.reshape(row_count, top_count, expert_count * capacity)
    picker = jnp.sum(hits, axis=1)
    weigher = jnp.sum(hits * gate_values[:, :, None], axis=1)
    return (picker, weigher)


def replica_sum(per_replica):
    total = jnp.zeros(per_replica.shape[1:], jnp.float32)
    for replica in range(per_replica.shape[0]):
        total = total + lax.optimization_barrier(per_replica[replica].astype(jnp.bfloat16)).astype(
            jnp.float32
        )
    return total


def renew(weights, grads, axis_number, rate):
    scale = jnp.sqrt(jnp.mean(grads * grads, axis=axis_number, keepdims=True) + EPSILON)
    return (weights.astype(jnp.float32) - rate * grads / scale).astype(jnp.bfloat16)


def forward_core(slot_rows, weights_gu, weights_dn):
    hidden_count = weights_gu.shape[2]
    both = jnp.dot(
        slot_rows,
        weights_gu.reshape(slot_rows.shape[1], 2 * hidden_count),
        preferred_element_type=jnp.float32,
    ).reshape(-1, 2, hidden_count)
    active = both[:, 0]
    upward = both[:, 1]
    hidden = (active * jax.nn.sigmoid(active) * upward).astype(jnp.bfloat16)
    return jnp.dot(hidden, weights_dn, preferred_element_type=jnp.float32).astype(jnp.bfloat16)


def learn_core(slot_rows, slot_grads, weights_gu, weights_dn, rep_count):
    slot_count, model_width = slot_rows.shape
    hidden_count = weights_gu.shape[2]
    both = jnp.dot(
        slot_rows,
        weights_gu.reshape(model_width, 2 * hidden_count),
        preferred_element_type=jnp.float32,
    ).reshape(slot_count, 2, hidden_count)
    active = both[:, 0]
    upward = both[:, 1]
    sigma = jax.nn.sigmoid(active)
    swish = active * sigma
    hidden = (swish * upward).astype(jnp.bfloat16)
    back = lax.dot_general(
        slot_grads, weights_dn, (((1,), (1,)), ((), ())), preferred_element_type=jnp.float32
    )
    d_active = back * upward * sigma * (1.0 + active * (1.0 - sigma))
    d_upward = back * swish
    d_both = jnp.stack([d_active, d_upward], axis=1).astype(jnp.bfloat16)
    grad_dn = jnp.einsum(
        "pch,pcd->phd",
        hidden.reshape(rep_count, -1, hidden_count),
        slot_grads.reshape(rep_count, -1, model_width),
        preferred_element_type=jnp.float32,
    )
    grad_gu = jnp.einsum(
        "pcd,pcgh->pdgh",
        slot_rows.reshape(rep_count, -1, model_width),
        d_both.reshape(rep_count, -1, 2, hidden_count),
        preferred_element_type=jnp.float32,
    )
    slot_dx = jnp.einsum("mgh,dgh->md", d_both, weights_gu, preferred_element_type=jnp.float32)
    slot_fw = jnp.dot(hidden, weights_dn, preferred_element_type=jnp.float32)
    return (grad_gu, grad_dn, slot_dx.astype(jnp.bfloat16), slot_fw.astype(jnp.bfloat16))


def per_device(
    rows_in,
    cotangent,
    lengths,
    train_experts,
    train_gates,
    decode_experts,
    decode_gates,
    gate_up,
    down,
):
    ep_count = lax.axis_size("ep")
    dp_count = lax.axis_size("dp")
    row_count, model_width = cotangent.shape
    top_count = train_experts.shape[1]
    capacity = min(row_count, max(2, 4 * row_count * top_count // (3 * ep_count)))
    is_learner = lax.axis_index("grp") == 0
    own_gu = gate_up[0, 0]
    own_dn = down[0, 0]
    hidden_all = own_gu.shape[2] * dp_count

    def spread(buffers, tag):
        return exchange(buffers, ep_count, tag, share=True)

    def bring_back(pieces, tag):
        half = pieces.shape[0] // dp_count
        mine = lax.axis_index("dp")
        keep = lax.dynamic_slice_in_dim(pieces, mine * half, half)
        give = lax.dynamic_slice_in_dim(pieces, (1 - mine) * half, half)
        got = lax.ppermute(give, "dp", [(0, 1), (1, 0)])
        summed = (keep.astype(jnp.float32) + got.astype(jnp.float32)).astype(jnp.bfloat16)
        return exchange([summed], ep_count, tag)[0]

    def combine(mixing, returned):
        total = returned.astype(jnp.float32)
        return jnp.einsum("rs,sd->rd", mixing, total, precision=lax.Precision.HIGHEST)

    def dispatch(picker, values):
        buffer = jnp.einsum(
            "rs,rd->sd", picker.astype(jnp.bfloat16), values, preferred_element_type=jnp.float32
        )
        return buffer.astype(jnp.bfloat16)

    tokens = rows_in[0]
    total_rows = row_count * ep_count * dp_count
    longest = 2 * total_rows // lengths.shape[0]
    first_row = (lax.axis_index("ep") * dp_count + lax.axis_index("dp")) * row_count
    places = first_row + jnp.arange(row_count, dtype=jnp.int32)
    ends = jnp.cumsum(lengths)
    starts = ends - lengths
    inside = (places[:, None] >= starts[None, :]) & (places[:, None] < ends[None, :])
    seq_len = jnp.sum(jnp.where(inside, lengths[None, :], 0), axis=1).astype(jnp.float32)
    weight = 2.0 * longest / (seq_len + longest)
    route_ids = jnp.where(is_learner, train_experts, decode_experts[0])
    route_gates = jnp.where(is_learner, train_gates, decode_gates[0])
    picker, weigher = routing_tables(route_ids, route_gates, capacity, ep_count)
    row_buffer = dispatch(picker, tokens)
    cot_wide = cotangent.astype(jnp.float32)
    grad_buffer = jnp.einsum(
        "rs,rd->sd", weigher * weight[:, None], cot_wide, precision=lax.Precision.HIGHEST
    ).astype(jnp.bfloat16)
    rows_got, grads_got = spread([row_buffer, grad_buffer], 0)
    per_gu, per_dn, slot_dx, slot_fw = learn_core(rows_got, grads_got, own_gu, own_dn, dp_count)
    grad_gu = replica_sum(per_gu)
    grad_dn = replica_sum(per_dn)
    returned = bring_back(jnp.where(is_learner, slot_dx, slot_fw), 1)
    mixing = jnp.where(is_learner, picker, weigher)
    base = jnp.where(is_learner, weight[:, None] * cot_wide, tokens.astype(jnp.float32))
    carried = (base + combine(mixing, returned)).astype(jnp.bfloat16)
    fresh_gu = renew(own_gu, grad_gu, 0, 0.5 / model_width**0.5)
    fresh_dn = renew(own_dn, grad_dn, 1, 0.5 / hidden_all**0.5)
    current = passed_along(carried, "grp", -1)
    picker, weigher = routing_tables(decode_experts[1], decode_gates[1], capacity, ep_count)
    (rows_got,) = spread([dispatch(picker, current)], 2)
    slot_out = forward_core(rows_got, fresh_gu, fresh_dn)
    returned = bring_back(slot_out, 3)
    current = (current.astype(jnp.float32) + combine(weigher, returned)).astype(jnp.bfloat16)
    final_rows = jnp.where(is_learner, carried, passed_along(current, "grp", 1))
    return final_rows[None]


def solution(mesh):
    placed = (
        P("grp", ("ep", "dp"), None),
        P(("ep", "dp"), None),
        P(),
        P(("ep", "dp"), None),
        P(("ep", "dp"), None),
        P(None, ("ep", "dp"), None),
        P(None, ("ep", "dp"), None),
        P("grp", "ep", None, None, "dp"),
        P("grp", "ep", "dp", None),
    )
    return jax.shard_map(
        per_device,
        mesh=mesh,
        in_specs=placed,
        out_specs=P("grp", ("ep", "dp"), None),
        check_vma=False,
    )
```

```python
import jax
import jax.numpy as jnp
from jax import lax
from jax.experimental import pallas as pl
from jax.experimental.pallas import tpu as pltpu
from jax.sharding import PartitionSpec as P
import functools

MESH = pl.DeviceIdType.MESH


def exchange_kernel(count, width, share, source, target, send_sem, recv_sem, own_sem):
    me = lax.axis_index("ep")
    rows = count * width
    side = lax.axis_index("dp")
    base = side * rows if share else 0
    barrier = pltpu.get_barrier_semaphore()

    def greet(k, carry):
        other = lax.rem(me + k, count)
        pl.semaphore_signal(barrier, inc=1, device_id={"ep": other}, device_id_type=MESH)
        return carry

    lax.fori_loop(1, count, greet, 0)
    if share:
        pl.semaphore_signal(barrier, inc=1, device_id={"dp": 1 - side}, device_id_type=MESH)
    pl.semaphore_wait(barrier, count - 1 + (1 if share else 0))

    def spot(index, start=0):
        return pl.ds(pl.multiple_of(start + index * width, width), width)

    own = pltpu.make_async_copy(
        source.at[:, spot(me)], target.at[:, spot(me, base)], own_sem.at[0]
    )
    own.start()

    def outgoing(k):
        step = jnp.where(k % 2 == 1, (k + 1) // 2, count - k // 2)
        other = lax.rem(me + step, count)
        return pltpu.make_async_remote_copy(
            src_ref=source.at[:, spot(other)],
            dst_ref=target.at[:, spot(me, base)],
            send_sem=send_sem.at[other],
            recv_sem=recv_sem.at[me],
            device_id={"ep": other},
            device_id_type=MESH,
        )

    def incoming(k):
        other = lax.rem(me + count - k, count)
        return pltpu.make_async_remote_copy(
            src_ref=source.at[:, spot(other)],
            dst_ref=target.at[:, spot(other, base)],
            send_sem=send_sem.at[other],
            recv_sem=recv_sem.at[other],
            device_id={"ep": other},
            device_id_type=MESH,
        )

    def launch(k, carry):
        outgoing(k).start()
        return carry

    lax.fori_loop(1, count, launch, 0)

    def settle(k, carry):
        outgoing(k).wait_send()
        return carry

    lax.fori_loop(1, count, settle, 0)

    def land(k, carry):
        incoming(k).wait_recv()
        return carry

    lax.fori_loop(1, count, land, 0)
    own.wait()
    if share:
        half = pl.ds(pl.multiple_of(base, rows), rows)
        yonder = pl.ds(pl.multiple_of((1 - side) * rows, rows), rows)
        onward = pltpu.make_async_remote_copy(
            src_ref=target.at[:, half],
            dst_ref=target.at[:, half],
            send_sem=own_sem.at[1],
            recv_sem=own_sem.at[2],
            device_id={"dp": 1 - side},
            device_id_type=MESH,
        )
        onward.start()
        onward.wait_send()
        pltpu.make_async_remote_copy(
            src_ref=target.at[:, yonder],
            dst_ref=target.at[:, yonder],
            send_sem=own_sem.at[1],
            recv_sem=own_sem.at[2],
            device_id={"dp": 1 - side},
            device_id_type=MESH,
        ).wait_recv()


def exchange(blocks, count, tag, share=False):
    block = jnp.stack(blocks)
    width = block.shape[1] // count
    grow = 2 if share else 1
    size = block.size * block.dtype.itemsize
    shape = (block.shape[0], grow * block.shape[1]) + block.shape[2:]
    merged = pl.pallas_call(
        functools.partial(exchange_kernel, count, width, share),
        out_shape=jax.ShapeDtypeStruct(shape, block.dtype),
        in_specs=[pl.BlockSpec(memory_space=pl.ANY)],
        out_specs=pl.BlockSpec(memory_space=pl.ANY),
        scratch_shapes=[
            pltpu.SemaphoreType.DMA((count,)),
            pltpu.SemaphoreType.DMA((count,)),
            pltpu.SemaphoreType.DMA((3,)),
        ],
        compiler_params=pltpu.CompilerParams(collective_id=tag, has_side_effects=True),
        cost_estimate=pl.CostEstimate(
            flops=0, transcendentals=0, bytes_accessed=(2 + 2 * grow) * size
        ),
    )(block)
    return [merged[index] for index in range(len(blocks))]


EPSILON = 1e-06


def passed_along(block, axis, distance):
    devices = range(lax.axis_size(axis))
    route = [(i - distance, i) for i in devices if i - distance in devices]
    return lax.ppermute(block, axis, route)


def routing_tables(expert_ids, gate_values, capacity, expert_count):
    row_count, top_count = expert_ids.shape
    flat_ids = expert_ids.reshape(row_count * top_count)
    onehot = (flat_ids[:, None] == jnp.arange(expert_count, dtype=jnp.int32)[None, :]).astype(
        jnp.int32
    )
    earlier = jnp.cumsum(onehot, axis=0) - onehot
    ranks = jnp.sum(earlier * onehot, axis=1)
    slots = flat_ids * capacity + ranks
    hits = (slots[:, None] == jnp.arange(expert_count * capacity, dtype=jnp.int32)[None, :]).astype(
        jnp.float32
    )
    hits = hits.reshape(row_count, top_count, expert_count * capacity)
    picker = jnp.sum(hits, axis=1)
    weigher = jnp.sum(hits * gate_values[:, :, None], axis=1)
    return (picker, weigher)


def replica_sum(per_replica):
    total = jnp.zeros(per_replica.shape[1:], jnp.float32)
    for replica in range(per_replica.shape[0]):
        total = total + lax.optimization_barrier(per_replica[replica].astype(jnp.bfloat16)).astype(
            jnp.float32
        )
    return total


def renew(weights, grads, axis_number, rate):
    scale = jnp.sqrt(jnp.mean(grads * grads, axis=axis_number, keepdims=True) + EPSILON)
    return (weights.astype(jnp.float32) - rate * grads / scale).astype(jnp.bfloat16)


def forward_core(slot_rows, weights_gu, weights_dn):
    hidden_count = weights_gu.shape[2]
    both = jnp.dot(
        slot_rows,
        weights_gu.reshape(slot_rows.shape[1], 2 * hidden_count),
        preferred_element_type=jnp.float32,
    ).reshape(-1, 2, hidden_count)
    active = both[:, 0]
    upward = both[:, 1]
    hidden = (active * jax.nn.sigmoid(active) * upward).astype(jnp.bfloat16)
    return jnp.dot(hidden, weights_dn, preferred_element_type=jnp.float32).astype(jnp.bfloat16)


def learn_core(slot_rows, slot_grads, weights_gu, weights_dn, rep_count):
    slot_count, model_width = slot_rows.shape
    hidden_count = weights_gu.shape[2]
    both = jnp.dot(
        slot_rows,
        weights_gu.reshape(model_width, 2 * hidden_count),
        preferred_element_type=jnp.float32,
    ).reshape(slot_count, 2, hidden_count)
    active = both[:, 0]
    upward = both[:, 1]
    sigma = jax.nn.sigmoid(active)
    swish = active * sigma
    hidden = (swish * upward).astype(jnp.bfloat16)
    back = lax.dot_general(
        slot_grads, weights_dn, (((1,), (1,)), ((), ())), preferred_element_type=jnp.float32
    )
    d_active = back * upward * sigma * (1.0 + active * (1.0 - sigma))
    d_upward = back * swish
    d_both = jnp.stack([d_active, d_upward], axis=1).astype(jnp.bfloat16)
    grad_dn = jnp.einsum(
        "pch,pcd->phd",
        hidden.reshape(rep_count, -1, hidden_count),
        slot_grads.reshape(rep_count, -1, model_width),
        preferred_element_type=jnp.float32,
    )
    grad_gu = jnp.einsum(
        "pcd,pcgh->pdgh",
        slot_rows.reshape(rep_count, -1, model_width),
        d_both.reshape(rep_count, -1, 2, hidden_count),
        preferred_element_type=jnp.float32,
    )
    slot_dx = jnp.einsum("mgh,dgh->md", d_both, weights_gu, preferred_element_type=jnp.float32)
    slot_fw = jnp.dot(hidden, weights_dn, preferred_element_type=jnp.float32)
    return (grad_gu, grad_dn, slot_dx.astype(jnp.bfloat16), slot_fw.astype(jnp.bfloat16))


def per_device(
    rows_in,
    cotangent,
    lengths,
    train_experts,
    train_gates,
    decode_experts,
    decode_gates,
    gate_up,
    down,
):
    ep_count = lax.axis_size("ep")
    dp_count = lax.axis_size("dp")
    row_count, model_width = cotangent.shape
    top_count = train_experts.shape[1]
    capacity = min(row_count, max(2, 4 * row_count * top_count // (3 * ep_count)))
    is_learner = lax.axis_index("grp") == 0
    own_gu = gate_up[0, 0]
    own_dn = down[0, 0]
    hidden_all = own_gu.shape[2] * dp_count

    def spread(buffers, tag):
        return exchange(buffers, ep_count, tag, share=True)

    def bring_back(pieces, tag):
        half = pieces.shape[0] // dp_count
        mine = lax.axis_index("dp")
        keep = lax.dynamic_slice_in_dim(pieces, mine * half, half)
        give = lax.dynamic_slice_in_dim(pieces, (1 - mine) * half, half)
        got = lax.ppermute(give, "dp", [(0, 1), (1, 0)])
        summed = (keep.astype(jnp.float32) + got.astype(jnp.float32)).astype(jnp.bfloat16)
        return exchange([summed], ep_count, tag)[0]

    def combine(mixing, returned):
        total = returned.astype(jnp.float32)
        return jnp.einsum("rs,sd->rd", mixing, total, precision=lax.Precision.HIGHEST)

    def dispatch(picker, values):
        buffer = jnp.einsum(
            "rs,rd->sd", picker.astype(jnp.bfloat16), values, preferred_element_type=jnp.float32
        )
        return buffer.astype(jnp.bfloat16)

    tokens = rows_in[0]
    total_rows = row_count * ep_count * dp_count
    longest = 2 * total_rows // lengths.shape[0]
    first_row = (lax.axis_index("ep") * dp_count + lax.axis_index("dp")) * row_count
    places = first_row + jnp.arange(row_count, dtype=jnp.int32)
    ends = jnp.cumsum(lengths)
    starts = ends - lengths
    inside = (places[:, None] >= starts[None, :]) & (places[:, None] < ends[None, :])
    seq_len = jnp.sum(jnp.where(inside, lengths[None, :], 0), axis=1).astype(jnp.float32)
    weight = 2.0 * longest / (seq_len + longest)
    route_ids = jnp.where(is_learner, train_experts, decode_experts[0])
    route_gates = jnp.where(is_learner, train_gates, decode_gates[0])
    picker, weigher = routing_tables(route_ids, route_gates, capacity, ep_count)
    row_buffer = dispatch(picker, tokens)
    cot_wide = cotangent.astype(jnp.float32)
    grad_buffer = jnp.einsum(
        "rs,rd->sd", weigher * weight[:, None], cot_wide, precision=lax.Precision.HIGHEST
    ).astype(jnp.bfloat16)
    rows_got, grads_got = spread([row_buffer, grad_buffer], 0)
    per_gu, per_dn, slot_dx, slot_fw = learn_core(rows_got, grads_got, own_gu, own_dn, dp_count)
    grad_gu = replica_sum(per_gu)
    grad_dn = replica_sum(per_dn)
    returned = bring_back(jnp.where(is_learner, slot_dx, slot_fw), 1)
    mixing = jnp.where(is_learner, picker, weigher)
    base = jnp.where(is_learner, weight[:, None] * cot_wide, tokens.astype(jnp.float32))
    carried = (base + combine(mixing, returned)).astype(jnp.bfloat16)
    fresh_gu = renew(own_gu, grad_gu, 0, 0.5 / model_width**0.5)
    fresh_dn = renew(own_dn, grad_dn, 1, 0.5 / hidden_all**0.5)
    current = passed_along(carried, "grp", -1)
    picker, weigher = routing_tables(decode_experts[1], decode_gates[1], capacity, ep_count)
    (rows_got,) = spread([dispatch(picker, current)], 2)
    slot_out = forward_core(rows_got, fresh_gu, fresh_dn)
    returned = bring_back(slot_out, 3)
    current = (current.astype(jnp.float32) + combine(weigher, returned)).astype(jnp.bfloat16)
    final_rows = jnp.where(is_learner, carried, passed_along(current, "grp", 1))
    return final_rows[None]


def solution(mesh):
    placed = (
        P("grp", ("ep", "dp"), None),
        P(("ep", "dp"), None),
        P(),
        P(("ep", "dp"), None),
        P(("ep", "dp"), None),
        P(None, ("ep", "dp"), None),
        P(None, ("ep", "dp"), None),
        P("grp", "ep", None, None, "dp"),
        P("grp", "ep", "dp", None),
    )
    return jax.shard_map(
        per_device,
        mesh=mesh,
        in_specs=placed,
        out_specs=P("grp", ("ep", "dp"), None),
        check_vma=False,
    )
```

```python
import jax
import jax.numpy as jnp
from jax import lax
from jax.experimental import pallas as pl
from jax.experimental.pallas import tpu as pltpu
from jax.sharding import PartitionSpec as P
import functools

MESH = pl.DeviceIdType.MESH


def exchange_kernel(count, width, share, *refs):
    parts = len(refs) // 2 - 1
    sources, targets = refs[:parts], refs[parts:2 * parts]
    send_sem, recv_sem, own_sem = refs[2 * parts:]
    me = lax.axis_index("ep")
    rows = count * width
    side = lax.axis_index("dp")
    base = side * rows if share else 0
    barrier = pltpu.get_barrier_semaphore()

    def greet(k, carry):
        other = lax.rem(me + k, count)
        pl.semaphore_signal(barrier, inc=1, device_id={"ep": other}, device_id_type=MESH)
        return carry

    lax.fori_loop(1, count, greet, 0)
    if share:
        pl.semaphore_signal(barrier, inc=1, device_id={"dp": 1 - side}, device_id_type=MESH)
    pl.semaphore_wait(barrier, count - 1 + (1 if share else 0))

    def spot(index, start=0):
        return pl.ds(pl.multiple_of(start + index * width, width), width)

    owns = []
    for part in range(parts):
        own = pltpu.make_async_copy(
            sources[part].at[spot(me)], targets[part].at[spot(me, base)], own_sem.at[part, 0]
        )
        own.start()
        owns.append(own)

    def outgoing(part, k):
        step = jnp.where(k % 2 == 1, (k + 1) // 2, count - k // 2)
        other = lax.rem(me + step, count)
        return pltpu.make_async_remote_copy(
            src_ref=sources[part].at[spot(other)],
            dst_ref=targets[part].at[spot(me, base)],
            send_sem=send_sem.at[part, other],
            recv_sem=recv_sem.at[part, me],
            device_id={"ep": other},
            device_id_type=MESH,
        )

    def incoming(part, k):
        other = lax.rem(me + count - k, count)
        return pltpu.make_async_remote_copy(
            src_ref=sources[part].at[spot(other)],
            dst_ref=targets[part].at[spot(other, base)],
            send_sem=send_sem.at[part, other],
            recv_sem=recv_sem.at[part, other],
            device_id={"ep": other},
            device_id_type=MESH,
        )

    def launch(k, carry):
        for part in range(parts):
            outgoing(part, k).start()
        return carry

    lax.fori_loop(1, count, launch, 0)

    def settle(k, carry):
        for part in range(parts):
            outgoing(part, k).wait_send()
        return carry

    lax.fori_loop(1, count, settle, 0)

    def land(k, carry):
        for part in range(parts):
            incoming(part, k).wait_recv()
        return carry

    lax.fori_loop(1, count, land, 0)
    for own in owns:
        own.wait()
    if share:
        half = pl.ds(pl.multiple_of(base, rows), rows)
        yonder = pl.ds(pl.multiple_of((1 - side) * rows, rows), rows)
        passes = []
        for part in range(parts):
            onward = pltpu.make_async_remote_copy(
                src_ref=targets[part].at[half],
                dst_ref=targets[part].at[half],
                send_sem=own_sem.at[part, 1],
                recv_sem=own_sem.at[part, 2],
                device_id={"dp": 1 - side},
                device_id_type=MESH,
            )
            onward.start()
            passes.append(onward)
        for part in range(parts):
            passes[part].wait_send()
            pltpu.make_async_remote_copy(
                src_ref=targets[part].at[yonder],
                dst_ref=targets[part].at[yonder],
                send_sem=own_sem.at[part, 1],
                recv_sem=own_sem.at[part, 2],
                device_id={"dp": 1 - side},
                device_id_type=MESH,
            ).wait_recv()


def exchange(blocks, count, tag, share=False):
    parts = len(blocks)
    width = blocks[0].shape[0] // count
    grow = 2 if share else 1
    size = sum(block.size * block.dtype.itemsize for block in blocks)
    return pl.pallas_call(
        functools.partial(exchange_kernel, count, width, share),
        out_shape=[
            jax.ShapeDtypeStruct((grow * block.shape[0],) + block.shape[1:], block.dtype)
            for block in blocks
        ],
        in_specs=[pl.BlockSpec(memory_space=pl.ANY)] * parts,
        out_specs=[pl.BlockSpec(memory_space=pl.ANY)] * parts,
        scratch_shapes=[
            pltpu.SemaphoreType.DMA((parts, count)),
            pltpu.SemaphoreType.DMA((parts, count)),
            pltpu.SemaphoreType.DMA((parts, 3)),
        ],
        compiler_params=pltpu.CompilerParams(collective_id=tag, has_side_effects=True),
        cost_estimate=pl.CostEstimate(
            flops=0, transcendentals=0, bytes_accessed=(2 + 2 * grow) * size
        ),
    )(*blocks)


def swap_kernel(source, target, send_sem, recv_sem):
    side = lax.axis_index("grp")
    barrier = pltpu.get_barrier_semaphore()
    pl.semaphore_signal(barrier, inc=1, device_id={"grp": 1 - side}, device_id_type=MESH)
    pl.semaphore_wait(barrier, 1)
    copy = pltpu.make_async_remote_copy(
        src_ref=source,
        dst_ref=target,
        send_sem=send_sem,
        recv_sem=recv_sem,
        device_id={"grp": 1 - side},
        device_id_type=MESH,
    )
    copy.start()
    copy.wait()


def swapped(block, tag):
    return pl.pallas_call(
        swap_kernel,
        out_shape=jax.ShapeDtypeStruct(block.shape, block.dtype),
        in_specs=[pl.BlockSpec(memory_space=pl.ANY)],
        out_specs=pl.BlockSpec(memory_space=pl.ANY),
        scratch_shapes=[pltpu.SemaphoreType.DMA(()), pltpu.SemaphoreType.DMA(())],
        compiler_params=pltpu.CompilerParams(collective_id=tag, has_side_effects=True),
    )(block)


EPSILON = 1e-06


def passed_along(block, axis, distance):
    devices = range(lax.axis_size(axis))
    route = [(i - distance, i) for i in devices if i - distance in devices]
    return lax.ppermute(block, axis, route)


def routing_tables(expert_ids, gate_values, capacity, expert_count):
    row_count, top_count = expert_ids.shape
    flat_ids = expert_ids.reshape(row_count * top_count)
    onehot = (flat_ids[:, None] == jnp.arange(expert_count, dtype=jnp.int32)[None, :]).astype(
        jnp.int32
    )
    earlier = jnp.cumsum(onehot, axis=0) - onehot
    ranks = jnp.sum(earlier * onehot, axis=1)
    slots = flat_ids * capacity + ranks
    hits = (slots[:, None] == jnp.arange(expert_count * capacity, dtype=jnp.int32)[None, :]).astype(
        jnp.float32
    )
    hits = hits.reshape(row_count, top_count, expert_count * capacity)
    picker = jnp.sum(hits, axis=1)
    weigher = jnp.sum(hits * gate_values[:, :, None], axis=1)
    return (picker, weigher)


def replica_sum(per_replica):
    total = jnp.zeros(per_replica.shape[1:], jnp.float32)
    for replica in range(per_replica.shape[0]):
        total = total + lax.optimization_barrier(per_replica[replica].astype(jnp.bfloat16)).astype(
            jnp.float32
        )
    return total


def renew(weights, grads, axis_number, rate):
    scale = jnp.sqrt(jnp.mean(grads * grads, axis=axis_number, keepdims=True) + EPSILON)
    return (weights.astype(jnp.float32) - rate * grads / scale).astype(jnp.bfloat16)


def forward_core(slot_rows, weights_gu, weights_dn):
    hidden_count = weights_gu.shape[2]
    both = jnp.dot(
        slot_rows,
        weights_gu.reshape(slot_rows.shape[1], 2 * hidden_count),
        preferred_element_type=jnp.float32,
    ).reshape(-1, 2, hidden_count)
    active = both[:, 0]
    upward = both[:, 1]
    hidden = (active * jax.nn.sigmoid(active) * upward).astype(jnp.bfloat16)
    return jnp.dot(hidden, weights_dn, preferred_element_type=jnp.float32).astype(jnp.bfloat16)


def learn_core(slot_rows, slot_grads, weights_gu, weights_dn, rep_count):
    slot_count, model_width = slot_rows.shape
    hidden_count = weights_gu.shape[2]
    both = jnp.dot(
        slot_rows,
        weights_gu.reshape(model_width, 2 * hidden_count),
        preferred_element_type=jnp.float32,
    ).reshape(slot_count, 2, hidden_count)
    active = both[:, 0]
    upward = both[:, 1]
    sigma = jax.nn.sigmoid(active)
    swish = active * sigma
    hidden = (swish * upward).astype(jnp.bfloat16)
    back = lax.dot_general(
        slot_grads, weights_dn, (((1,), (1,)), ((), ())), preferred_element_type=jnp.float32
    )
    d_active = back * upward * sigma * (1.0 + active * (1.0 - sigma))
    d_upward = back * swish
    d_both = jnp.stack([d_active, d_upward], axis=1).astype(jnp.bfloat16)
    grad_dn = jnp.einsum(
        "pch,pcd->phd",
        hidden.reshape(rep_count, -1, hidden_count),
        slot_grads.reshape(rep_count, -1, model_width),
        preferred_element_type=jnp.float32,
    )
    grad_gu = jnp.einsum(
        "pcd,pcgh->pdgh",
        slot_rows.reshape(rep_count, -1, model_width),
        d_both.reshape(rep_count, -1, 2, hidden_count),
        preferred_element_type=jnp.float32,
    )
    slot_dx = jnp.einsum("mgh,dgh->md", d_both, weights_gu, preferred_element_type=jnp.float32)
    slot_fw = jnp.dot(hidden, weights_dn, preferred_element_type=jnp.float32)
    return (grad_gu, grad_dn, slot_dx.astype(jnp.bfloat16), slot_fw.astype(jnp.bfloat16))


def per_device(
    rows_in,
    cotangent,
    lengths,
    train_experts,
    train_gates,
    decode_experts,
    decode_gates,
    gate_up,
    down,
):
    ep_count = lax.axis_size("ep")
    dp_count = lax.axis_size("dp")
    row_count, model_width = cotangent.shape
    top_count = train_experts.shape[1]
    capacity = min(row_count, max(2, 4 * row_count * top_count // (3 * ep_count)))
    is_learner = lax.axis_index("grp") == 0
    own_gu = gate_up[0, 0]
    own_dn = down[0, 0]
    hidden_all = own_gu.shape[2] * dp_count

    def spread(buffers, tag):
        return exchange(buffers, ep_count, tag, share=True)

    def bring_back(pieces, tag):
        half = pieces.shape[0] // dp_count
        mine = lax.axis_index("dp")
        keep = lax.dynamic_slice_in_dim(pieces, mine * half, half)
        give = lax.dynamic_slice_in_dim(pieces, (1 - mine) * half, half)
        got = lax.ppermute(give, "dp", [(0, 1), (1, 0)])
        summed = (keep.astype(jnp.float32) + got.astype(jnp.float32)).astype(jnp.bfloat16)
        return exchange([summed], ep_count, tag)[0]

    def combine(mixing, returned):
        total = returned.astype(jnp.float32)
        return jnp.einsum("rs,sd->rd", mixing, total, precision=lax.Precision.HIGHEST)

    def dispatch(picker, values):
        buffer = jnp.einsum(
            "rs,rd->sd", picker.astype(jnp.bfloat16), values, preferred_element_type=jnp.float32
        )
        return buffer.astype(jnp.bfloat16)

    tokens = rows_in[0]
    total_rows = row_count * ep_count * dp_count
    longest = 2 * total_rows // lengths.shape[0]
    first_row = (lax.axis_index("ep") * dp_count + lax.axis_index("dp")) * row_count
    places = first_row + jnp.arange(row_count, dtype=jnp.int32)
    ends = jnp.cumsum(lengths)
    starts = ends - lengths
    inside = (places[:, None] >= starts[None, :]) & (places[:, None] < ends[None, :])
    seq_len = jnp.sum(jnp.where(inside, lengths[None, :], 0), axis=1).astype(jnp.float32)
    weight = 2.0 * longest / (seq_len + longest)
    route_ids = jnp.where(is_learner, train_experts, decode_experts[0])
    route_gates = jnp.where(is_learner, train_gates, decode_gates[0])
    picker, weigher = routing_tables(route_ids, route_gates, capacity, ep_count)
    row_buffer = dispatch(picker, tokens)
    cot_wide = cotangent.astype(jnp.float32)
    grad_buffer = jnp.einsum(
        "rs,rd->sd", weigher * weight[:, None], cot_wide, precision=lax.Precision.HIGHEST
    ).astype(jnp.bfloat16)
    rows_got, grads_got = spread([row_buffer, grad_buffer], 0)
    per_gu, per_dn, slot_dx, slot_fw = learn_core(rows_got, grads_got, own_gu, own_dn, dp_count)
    grad_gu = replica_sum(per_gu)
    grad_dn = replica_sum(per_dn)
    returned = bring_back(jnp.where(is_learner, slot_dx, slot_fw), 1)
    mixing = jnp.where(is_learner, picker, weigher)
    base = jnp.where(is_learner, weight[:, None] * cot_wide, tokens.astype(jnp.float32))
    carried = (base + combine(mixing, returned)).astype(jnp.bfloat16)
    fresh_gu = renew(own_gu, grad_gu, 0, 0.5 / model_width**0.5)
    fresh_dn = renew(own_dn, grad_dn, 1, 0.5 / hidden_all**0.5)
    current = swapped(carried, 4)
    picker, weigher = routing_tables(decode_experts[1], decode_gates[1], capacity, ep_count)
    (rows_got,) = spread([dispatch(picker, current)], 2)
    slot_out = forward_core(rows_got, fresh_gu, fresh_dn)
    returned = bring_back(slot_out, 3)
    current = (current.astype(jnp.float32) + combine(weigher, returned)).astype(jnp.bfloat16)
    final_rows = jnp.where(is_learner, carried, swapped(current, 5))
    return final_rows[None]


def solution(mesh):
    placed = (
        P("grp", ("ep", "dp"), None),
        P(("ep", "dp"), None),
        P(),
        P(("ep", "dp"), None),
        P(("ep", "dp"), None),
        P(None, ("ep", "dp"), None),
        P(None, ("ep", "dp"), None),
        P("grp", "ep", None, None, "dp"),
        P("grp", "ep", "dp", None),
    )
    return jax.shard_map(
        per_device,
        mesh=mesh,
        in_specs=placed,
        out_specs=P("grp", ("ep", "dp"), None),
        check_vma=False,
    )
```

```python
import jax
import jax.numpy as jnp
from jax import lax
from jax.experimental import pallas as pl
from jax.experimental.pallas import tpu as pltpu
from jax.sharding import PartitionSpec as P
import functools

MESH = pl.DeviceIdType.MESH


def exchange_kernel(count, width, share, *refs):
    parts = len(refs) // 2 - 1
    sources, targets = refs[:parts], refs[parts:2 * parts]
    send_sem, recv_sem, own_sem = refs[2 * parts:]
    me = lax.axis_index("ep")
    rows = count * width
    side = lax.axis_index("dp")
    base = side * rows if share else 0
    barrier = pltpu.get_barrier_semaphore()

    def greet(k, carry):
        other = lax.rem(me + k, count)
        pl.semaphore_signal(barrier, inc=1, device_id={"ep": other}, device_id_type=MESH)
        return carry

    lax.fori_loop(1, count, greet, 0)
    if share:
        pl.semaphore_signal(barrier, inc=1, device_id={"dp": 1 - side}, device_id_type=MESH)
    pl.semaphore_wait(barrier, count - 1 + (1 if share else 0))

    def spot(index, start=0):
        return pl.ds(pl.multiple_of(start + index * width, width), width)

    owns = []
    for part in range(parts):
        own = pltpu.make_async_copy(
            sources[part].at[spot(me)], targets[part].at[spot(me, base)], own_sem.at[part, 0]
        )
        own.start()
        owns.append(own)

    def outgoing(part, k):
        step = jnp.where(k % 2 == 1, (k + 1) // 2, count - k // 2)
        other = lax.rem(me + step, count)
        return pltpu.make_async_remote_copy(
            src_ref=sources[part].at[spot(other)],
            dst_ref=targets[part].at[spot(me, base)],
            send_sem=send_sem.at[part, other],
            recv_sem=recv_sem.at[part, me],
            device_id={"ep": other},
            device_id_type=MESH,
        )

    def incoming(part, k):
        other = lax.rem(me + count - k, count)
        return pltpu.make_async_remote_copy(
            src_ref=sources[part].at[spot(other)],
            dst_ref=targets[part].at[spot(other, base)],
            send_sem=send_sem.at[part, other],
            recv_sem=recv_sem.at[part, other],
            device_id={"ep": other},
            device_id_type=MESH,
        )

    def launch(k, carry):
        for part in range(parts):
            outgoing(part, k).start()
        return carry

    lax.fori_loop(1, count, launch, 0)

    def settle(k, carry):
        for part in range(parts):
            outgoing(part, k).wait_send()
        return carry

    lax.fori_loop(1, count, settle, 0)

    def land(k, carry):
        for part in range(parts):
            incoming(part, k).wait_recv()
        return carry

    lax.fori_loop(1, count, land, 0)
    for own in owns:
        own.wait()
    if share:
        half = pl.ds(pl.multiple_of(base, rows), rows)
        yonder = pl.ds(pl.multiple_of((1 - side) * rows, rows), rows)
        passes = []
        for part in range(parts):
            onward = pltpu.make_async_remote_copy(
                src_ref=targets[part].at[half],
                dst_ref=targets[part].at[half],
                send_sem=own_sem.at[part, 1],
                recv_sem=own_sem.at[part, 2],
                device_id={"dp": 1 - side},
                device_id_type=MESH,
            )
            onward.start()
            passes.append(onward)
        for part in range(parts):
            passes[part].wait_send()
            pltpu.make_async_remote_copy(
                src_ref=targets[part].at[yonder],
                dst_ref=targets[part].at[yonder],
                send_sem=own_sem.at[part, 1],
                recv_sem=own_sem.at[part, 2],
                device_id={"dp": 1 - side},
                device_id_type=MESH,
            ).wait_recv()


def exchange(blocks, count, tag, share=False):
    parts = len(blocks)
    width = blocks[0].shape[0] // count
    grow = 2 if share else 1
    size = sum(block.size * block.dtype.itemsize for block in blocks)
    return pl.pallas_call(
        functools.partial(exchange_kernel, count, width, share),
        out_shape=[
            jax.ShapeDtypeStruct((grow * block.shape[0],) + block.shape[1:], block.dtype)
            for block in blocks
        ],
        in_specs=[pl.BlockSpec(memory_space=pl.ANY)] * parts,
        out_specs=[pl.BlockSpec(memory_space=pl.ANY)] * parts,
        scratch_shapes=[
            pltpu.SemaphoreType.DMA((parts, count)),
            pltpu.SemaphoreType.DMA((parts, count)),
            pltpu.SemaphoreType.DMA((parts, 3)),
        ],
        compiler_params=pltpu.CompilerParams(collective_id=tag, has_side_effects=True),
        cost_estimate=pl.CostEstimate(
            flops=0, transcendentals=0, bytes_accessed=(2 + 2 * grow) * size
        ),
    )(*blocks)


EPSILON = 1e-06


def passed_along(block, axis, distance):
    devices = range(lax.axis_size(axis))
    route = [(i - distance, i) for i in devices if i - distance in devices]
    return lax.ppermute(block, axis, route)


def routing_tables(expert_ids, gate_values, capacity, expert_count):
    row_count, top_count = expert_ids.shape
    flat_ids = expert_ids.reshape(row_count * top_count)
    onehot = (flat_ids[:, None] == jnp.arange(expert_count, dtype=jnp.int32)[None, :]).astype(
        jnp.int32
    )
    earlier = jnp.cumsum(onehot, axis=0) - onehot
    ranks = jnp.sum(earlier * onehot, axis=1)
    slots = flat_ids * capacity + ranks
    hits = (slots[:, None] == jnp.arange(expert_count * capacity, dtype=jnp.int32)[None, :]).astype(
        jnp.float32
    )
    hits = hits.reshape(row_count, top_count, expert_count * capacity)
    picker = jnp.sum(hits, axis=1)
    weigher = jnp.sum(hits * gate_values[:, :, None], axis=1)
    return (picker, weigher)


def replica_sum(per_replica):
    total = jnp.zeros(per_replica.shape[1:], jnp.float32)
    for replica in range(per_replica.shape[0]):
        total = total + lax.optimization_barrier(per_replica[replica].astype(jnp.bfloat16)).astype(
            jnp.float32
        )
    return total


def renew(weights, grads, axis_number, rate):
    scale = jnp.sqrt(jnp.mean(grads * grads, axis=axis_number, keepdims=True) + EPSILON)
    return (weights.astype(jnp.float32) - rate * grads / scale).astype(jnp.bfloat16)


def forward_core(slot_rows, weights_gu, weights_dn):
    hidden_count = weights_gu.shape[2]
    both = jnp.dot(
        slot_rows,
        weights_gu.reshape(slot_rows.shape[1], 2 * hidden_count),
        preferred_element_type=jnp.float32,
    ).reshape(-1, 2, hidden_count)
    active = both[:, 0]
    upward = both[:, 1]
    hidden = (active * jax.nn.sigmoid(active) * upward).astype(jnp.bfloat16)
    return jnp.dot(hidden, weights_dn, preferred_element_type=jnp.float32).astype(jnp.bfloat16)


def learn_core(slot_rows, slot_grads, weights_gu, weights_dn, rep_count):
    slot_count, model_width = slot_rows.shape
    hidden_count = weights_gu.shape[2]
    both = jnp.dot(
        slot_rows,
        weights_gu.reshape(model_width, 2 * hidden_count),
        preferred_element_type=jnp.float32,
    ).reshape(slot_count, 2, hidden_count)
    active = both[:, 0]
    upward = both[:, 1]
    sigma = jax.nn.sigmoid(active)
    swish = active * sigma
    hidden = (swish * upward).astype(jnp.bfloat16)
    back = lax.dot_general(
        slot_grads, weights_dn, (((1,), (1,)), ((), ())), preferred_element_type=jnp.float32
    )
    d_active = back * upward * sigma * (1.0 + active * (1.0 - sigma))
    d_upward = back * swish
    d_both = jnp.stack([d_active, d_upward], axis=1).astype(jnp.bfloat16)
    grad_dn = jnp.einsum(
        "pch,pcd->phd",
        hidden.reshape(rep_count, -1, hidden_count),
        slot_grads.reshape(rep_count, -1, model_width),
        preferred_element_type=jnp.float32,
    )
    grad_gu = jnp.einsum(
        "pcd,pcgh->pdgh",
        slot_rows.reshape(rep_count, -1, model_width),
        d_both.reshape(rep_count, -1, 2, hidden_count),
        preferred_element_type=jnp.float32,
    )
    slot_dx = jnp.einsum("mgh,dgh->md", d_both, weights_gu, preferred_element_type=jnp.float32)
    slot_fw = jnp.dot(hidden, weights_dn, preferred_element_type=jnp.float32)
    return (grad_gu, grad_dn, slot_dx.astype(jnp.bfloat16), slot_fw.astype(jnp.bfloat16))


def per_device(
    rows_in,
    cotangent,
    lengths,
    train_experts,
    train_gates,
    decode_experts,
    decode_gates,
    gate_up,
    down,
):
    ep_count = lax.axis_size("ep")
    dp_count = lax.axis_size("dp")
    row_count, model_width = cotangent.shape
    top_count = train_experts.shape[1]
    capacity = min(row_count, max(2, 4 * row_count * top_count // (3 * ep_count)))
    is_learner = lax.axis_index("grp") == 0
    own_gu = gate_up[0, 0]
    own_dn = down[0, 0]
    hidden_all = own_gu.shape[2] * dp_count

    def spread(buffers, tag):
        return exchange(buffers, ep_count, tag, share=True)

    def bring_back(pieces, tag):
        half = pieces.shape[0] // dp_count
        mine = lax.axis_index("dp")
        keep = lax.dynamic_slice_in_dim(pieces, mine * half, half)
        give = lax.dynamic_slice_in_dim(pieces, (1 - mine) * half, half)
        got = lax.ppermute(give, "dp", [(0, 1), (1, 0)])
        summed = (keep.astype(jnp.float32) + got.astype(jnp.float32)).astype(jnp.bfloat16)
        return exchange([summed], ep_count, tag)[0]

    def combine(mixing, returned):
        total = returned.astype(jnp.float32)
        return jnp.einsum("rs,sd->rd", mixing, total, precision=lax.Precision.HIGHEST)

    def dispatch(picker, values):
        buffer = jnp.einsum(
            "rs,rd->sd", picker.astype(jnp.bfloat16), values, preferred_element_type=jnp.float32
        )
        return buffer.astype(jnp.bfloat16)

    tokens = rows_in[0]
    total_rows = row_count * ep_count * dp_count
    longest = 2 * total_rows // lengths.shape[0]
    first_row = (lax.axis_index("ep") * dp_count + lax.axis_index("dp")) * row_count
    places = first_row + jnp.arange(row_count, dtype=jnp.int32)
    ends = jnp.cumsum(lengths)
    starts = ends - lengths
    inside = (places[:, None] >= starts[None, :]) & (places[:, None] < ends[None, :])
    seq_len = jnp.sum(jnp.where(inside, lengths[None, :], 0), axis=1).astype(jnp.float32)
    weight = 2.0 * longest / (seq_len + longest)
    route_ids = jnp.where(is_learner, train_experts, decode_experts[0])
    route_gates = jnp.where(is_learner, train_gates, decode_gates[0])
    picker, weigher = routing_tables(route_ids, route_gates, capacity, ep_count)
    row_buffer = dispatch(picker, tokens)
    cot_wide = cotangent.astype(jnp.float32)
    grad_buffer = jnp.einsum(
        "rs,rd->sd", weigher * weight[:, None], cot_wide, precision=lax.Precision.HIGHEST
    ).astype(jnp.bfloat16)
    rows_got, grads_got = spread([row_buffer, grad_buffer], 0)

    def learner_side(rows_got, grads_got):
        per_gu, per_dn, slot_dx, _ = learn_core(rows_got, grads_got, own_gu, own_dn, dp_count)
        grad_gu = replica_sum(per_gu)
        grad_dn = replica_sum(per_dn)
        fresh_gu = renew(own_gu, grad_gu, 0, 0.5 / model_width**0.5)
        fresh_dn = renew(own_dn, grad_dn, 1, 0.5 / hidden_all**0.5)
        return (slot_dx, fresh_gu, fresh_dn)

    def rollout_side(rows_got, grads_got):
        return (forward_core(rows_got, own_gu, own_dn), own_gu, own_dn)

    pieces, fresh_gu, fresh_dn = lax.cond(
        is_learner, learner_side, rollout_side, rows_got, grads_got
    )
    returned = bring_back(pieces, 1)
    mixing = jnp.where(is_learner, picker, weigher)
    base = jnp.where(is_learner, weight[:, None] * cot_wide, tokens.astype(jnp.float32))
    carried = (base + combine(mixing, returned)).astype(jnp.bfloat16)
    picker, weigher = routing_tables(decode_experts[1], decode_gates[1], capacity, ep_count)

    def learner_wait(carried):
        return jnp.zeros((ep_count * capacity, model_width), jnp.bfloat16)

    def rollout_send(carried):
        return exchange([dispatch(picker, carried)], ep_count, 2)[0]

    half_rows = lax.cond(is_learner, learner_wait, rollout_send, carried)
    current = passed_along(carried, "grp", -1)
    half_rows = passed_along(half_rows, "grp", -1)
    other_rows = lax.ppermute(half_rows, "dp", [(0, 1), (1, 0)])
    rows_got = jnp.where(
        lax.axis_index("dp") == 0,
        jnp.concatenate([half_rows, other_rows], axis=0),
        jnp.concatenate([other_rows, half_rows], axis=0),
    )
    slot_out = forward_core(rows_got, fresh_gu, fresh_dn)
    returned = bring_back(slot_out, 3)
    current = (current.astype(jnp.float32) + combine(weigher, returned)).astype(jnp.bfloat16)
    final_rows = jnp.where(is_learner, carried, passed_along(current, "grp", 1))
    return final_rows[None]


def solution(mesh):
    placed = (
        P("grp", ("ep", "dp"), None),
        P(("ep", "dp"), None),
        P(),
        P(("ep", "dp"), None),
        P(("ep", "dp"), None),
        P(None, ("ep", "dp"), None),
        P(None, ("ep", "dp"), None),
        P("grp", "ep", None, None, "dp"),
        P("grp", "ep", "dp", None),
    )
    return jax.shard_map(
        per_device,
        mesh=mesh,
        in_specs=placed,
        out_specs=P("grp", ("ep", "dp"), None),
        check_vma=False,
    )
```

```python
import jax
import jax.numpy as jnp
from jax import lax
from jax.experimental import pallas as pl
from jax.experimental.pallas import tpu as pltpu
from jax.sharding import PartitionSpec as P
import functools

MESH = pl.DeviceIdType.MESH


def exchange_kernel(count, width, share, *refs):
    parts = len(refs) // 2 - 1
    sources, targets = refs[:parts], refs[parts:2 * parts]
    send_sem, recv_sem, own_sem = refs[2 * parts:]
    me = lax.axis_index("ep")
    rows = count * width
    side = lax.axis_index("dp")
    base = side * rows if share else 0
    barrier = pltpu.get_barrier_semaphore()

    def greet(k, carry):
        other = lax.rem(me + k, count)
        pl.semaphore_signal(barrier, inc=1, device_id={"ep": other}, device_id_type=MESH)
        return carry

    lax.fori_loop(1, count, greet, 0)
    if share:
        pl.semaphore_signal(barrier, inc=1, device_id={"dp": 1 - side}, device_id_type=MESH)
    pl.semaphore_wait(barrier, count - 1 + (1 if share else 0))

    def spot(index, start=0):
        return pl.ds(pl.multiple_of(start + index * width, width), width)

    owns = []
    for part in range(parts):
        own = pltpu.make_async_copy(
            sources[part].at[spot(me)], targets[part].at[spot(me, base)], own_sem.at[part, 0]
        )
        own.start()
        owns.append(own)

    def outgoing(part, k):
        step = jnp.where(k % 2 == 1, (k + 1) // 2, count - k // 2)
        other = lax.rem(me + step, count)
        return pltpu.make_async_remote_copy(
            src_ref=sources[part].at[spot(other)],
            dst_ref=targets[part].at[spot(me, base)],
            send_sem=send_sem.at[part, other],
            recv_sem=recv_sem.at[part, me],
            device_id={"ep": other},
            device_id_type=MESH,
        )

    def incoming(part, k):
        other = lax.rem(me + count - k, count)
        return pltpu.make_async_remote_copy(
            src_ref=sources[part].at[spot(other)],
            dst_ref=targets[part].at[spot(other, base)],
            send_sem=send_sem.at[part, other],
            recv_sem=recv_sem.at[part, other],
            device_id={"ep": other},
            device_id_type=MESH,
        )

    def launch(k, carry):
        for part in range(parts):
            outgoing(part, k).start()
        return carry

    lax.fori_loop(1, count, launch, 0)

    def settle(k, carry):
        for part in range(parts):
            outgoing(part, k).wait_send()
        return carry

    lax.fori_loop(1, count, settle, 0)

    def land(k, carry):
        for part in range(parts):
            incoming(part, k).wait_recv()
        return carry

    lax.fori_loop(1, count, land, 0)
    for own in owns:
        own.wait()
    if share:
        half = pl.ds(pl.multiple_of(base, rows), rows)
        yonder = pl.ds(pl.multiple_of((1 - side) * rows, rows), rows)
        passes = []
        for part in range(parts):
            onward = pltpu.make_async_remote_copy(
                src_ref=targets[part].at[half],
                dst_ref=targets[part].at[half],
                send_sem=own_sem.at[part, 1],
                recv_sem=own_sem.at[part, 2],
                device_id={"dp": 1 - side},
                device_id_type=MESH,
            )
            onward.start()
            passes.append(onward)
        for part in range(parts):
            passes[part].wait_send()
            pltpu.make_async_remote_copy(
                src_ref=targets[part].at[yonder],
                dst_ref=targets[part].at[yonder],
                send_sem=own_sem.at[part, 1],
                recv_sem=own_sem.at[part, 2],
                device_id={"dp": 1 - side},
                device_id_type=MESH,
            ).wait_recv()


def exchange(blocks, count, tag, share=False):
    parts = len(blocks)
    width = blocks[0].shape[0] // count
    grow = 2 if share else 1
    size = sum(block.size * block.dtype.itemsize for block in blocks)
    return pl.pallas_call(
        functools.partial(exchange_kernel, count, width, share),
        out_shape=[
            jax.ShapeDtypeStruct((grow * block.shape[0],) + block.shape[1:], block.dtype)
            for block in blocks
        ],
        in_specs=[pl.BlockSpec(memory_space=pl.ANY)] * parts,
        out_specs=[pl.BlockSpec(memory_space=pl.ANY)] * parts,
        scratch_shapes=[
            pltpu.SemaphoreType.DMA((parts, count)),
            pltpu.SemaphoreType.DMA((parts, count)),
            pltpu.SemaphoreType.DMA((parts, 3)),
        ],
        compiler_params=pltpu.CompilerParams(collective_id=tag, has_side_effects=True),
        cost_estimate=pl.CostEstimate(
            flops=0, transcendentals=0, bytes_accessed=(2 + 2 * grow) * size
        ),
    )(*blocks)


EPSILON = 1e-06


def passed_along(block, axis, distance):
    devices = range(lax.axis_size(axis))
    route = [(i - distance, i) for i in devices if i - distance in devices]
    return lax.ppermute(block, axis, route)


def routing_tables(expert_ids, gate_values, capacity, expert_count):
    row_count, top_count = expert_ids.shape
    flat_ids = expert_ids.reshape(row_count * top_count)
    onehot = (flat_ids[:, None] == jnp.arange(expert_count, dtype=jnp.int32)[None, :]).astype(
        jnp.int32
    )
    earlier = jnp.cumsum(onehot, axis=0) - onehot
    ranks = jnp.sum(earlier * onehot, axis=1)
    slots = flat_ids * capacity + ranks
    hits = (slots[:, None] == jnp.arange(expert_count * capacity, dtype=jnp.int32)[None, :]).astype(
        jnp.float32
    )
    hits = hits.reshape(row_count, top_count, expert_count * capacity)
    picker = jnp.sum(hits, axis=1)
    weigher = jnp.sum(hits * gate_values[:, :, None], axis=1)
    return (picker, weigher)


def replica_sum(per_replica):
    total = jnp.zeros(per_replica.shape[1:], jnp.float32)
    for replica in range(per_replica.shape[0]):
        total = total + lax.optimization_barrier(per_replica[replica].astype(jnp.bfloat16)).astype(
            jnp.float32
        )
    return total


def renew(weights, grads, axis_number, rate):
    scale = jnp.sqrt(jnp.mean(grads * grads, axis=axis_number, keepdims=True) + EPSILON)
    return (weights.astype(jnp.float32) - rate * grads / scale).astype(jnp.bfloat16)


def forward_core(slot_rows, weights_gu, weights_dn):
    hidden_count = weights_gu.shape[2]
    both = jnp.dot(
        slot_rows,
        weights_gu.reshape(slot_rows.shape[1], 2 * hidden_count),
        preferred_element_type=jnp.float32,
    ).reshape(-1, 2, hidden_count)
    active = both[:, 0]
    upward = both[:, 1]
    hidden = (active * jax.nn.sigmoid(active) * upward).astype(jnp.bfloat16)
    return jnp.dot(hidden, weights_dn, preferred_element_type=jnp.float32).astype(jnp.bfloat16)


def learn_core(slot_rows, slot_grads, weights_gu, weights_dn, rep_count):
    slot_count, model_width = slot_rows.shape
    hidden_count = weights_gu.shape[2]
    both = jnp.dot(
        slot_rows,
        weights_gu.reshape(model_width, 2 * hidden_count),
        preferred_element_type=jnp.float32,
    ).reshape(slot_count, 2, hidden_count)
    active = both[:, 0]
    upward = both[:, 1]
    sigma = jax.nn.sigmoid(active)
    swish = active * sigma
    hidden = (swish * upward).astype(jnp.bfloat16)
    back = lax.dot_general(
        slot_grads, weights_dn, (((1,), (1,)), ((), ())), preferred_element_type=jnp.float32
    )
    d_active = back * upward * sigma * (1.0 + active * (1.0 - sigma))
    d_upward = back * swish
    d_both = jnp.stack([d_active, d_upward], axis=1).astype(jnp.bfloat16)
    grad_dn = jnp.einsum(
        "pch,pcd->phd",
        hidden.reshape(rep_count, -1, hidden_count),
        slot_grads.reshape(rep_count, -1, model_width),
        preferred_element_type=jnp.float32,
    )
    grad_gu = jnp.einsum(
        "pcd,pcgh->pdgh",
        slot_rows.reshape(rep_count, -1, model_width),
        d_both.reshape(rep_count, -1, 2, hidden_count),
        preferred_element_type=jnp.float32,
    )
    slot_dx = jnp.einsum("mgh,dgh->md", d_both, weights_gu, preferred_element_type=jnp.float32)
    slot_fw = jnp.dot(hidden, weights_dn, preferred_element_type=jnp.float32)
    return (grad_gu, grad_dn, slot_dx.astype(jnp.bfloat16), slot_fw.astype(jnp.bfloat16))


def per_device(
    rows_in,
    cotangent,
    lengths,
    train_experts,
    train_gates,
    decode_experts,
    decode_gates,
    gate_up,
    down,
):
    ep_count = lax.axis_size("ep")
    dp_count = lax.axis_size("dp")
    row_count, model_width = cotangent.shape
    top_count = train_experts.shape[1]
    capacity = min(row_count, max(2, 4 * row_count * top_count // (3 * ep_count)))
    is_learner = lax.axis_index("grp") == 0
    own_gu = gate_up[0, 0]
    own_dn = down[0, 0]
    hidden_all = own_gu.shape[2] * dp_count

    def spread(buffers, tag):
        return exchange(buffers, ep_count, tag, share=True)

    def bring_back(pieces, tag):
        half = pieces.shape[0] // dp_count
        mine = lax.axis_index("dp")
        keep = lax.dynamic_slice_in_dim(pieces, mine * half, half)
        give = lax.dynamic_slice_in_dim(pieces, (1 - mine) * half, half)
        got = lax.ppermute(give, "dp", [(0, 1), (1, 0)])
        summed = (keep.astype(jnp.float32) + got.astype(jnp.float32)).astype(jnp.bfloat16)
        return exchange([summed], ep_count, tag)[0]

    def combine(mixing, returned):
        high = mixing.astype(jnp.bfloat16)
        low = (mixing - high.astype(jnp.float32)).astype(jnp.bfloat16)
        return jnp.dot(high, returned, preferred_element_type=jnp.float32) + jnp.dot(
            low, returned, preferred_element_type=jnp.float32
        )

    def dispatch(picker, values):
        buffer = jnp.einsum(
            "rs,rd->sd", picker.astype(jnp.bfloat16), values, preferred_element_type=jnp.float32
        )
        return buffer.astype(jnp.bfloat16)

    tokens = rows_in[0]
    total_rows = row_count * ep_count * dp_count
    longest = 2 * total_rows // lengths.shape[0]
    first_row = (lax.axis_index("ep") * dp_count + lax.axis_index("dp")) * row_count
    places = first_row + jnp.arange(row_count, dtype=jnp.int32)
    ends = jnp.cumsum(lengths)
    starts = ends - lengths
    inside = (places[:, None] >= starts[None, :]) & (places[:, None] < ends[None, :])
    seq_len = jnp.sum(jnp.where(inside, lengths[None, :], 0), axis=1).astype(jnp.float32)
    weight = 2.0 * longest / (seq_len + longest)
    route_ids = jnp.where(is_learner, train_experts, decode_experts[0])
    route_gates = jnp.where(is_learner, train_gates, decode_gates[0])
    picker, weigher = routing_tables(route_ids, route_gates, capacity, ep_count)
    row_buffer = dispatch(picker, tokens)
    cot_wide = cotangent.astype(jnp.float32)
    scaled = weigher * weight[:, None]
    scaled_high = scaled.astype(jnp.bfloat16)
    scaled_low = (scaled - scaled_high.astype(jnp.float32)).astype(jnp.bfloat16)
    grad_buffer = (
        jnp.einsum("rs,rd->sd", scaled_high, cotangent, preferred_element_type=jnp.float32)
        + jnp.einsum("rs,rd->sd", scaled_low, cotangent, preferred_element_type=jnp.float32)
    ).astype(jnp.bfloat16)
    rows_got, grads_got = spread([row_buffer, grad_buffer], 0)
    per_gu, per_dn, slot_dx, slot_fw = learn_core(rows_got, grads_got, own_gu, own_dn, dp_count)
    grad_gu = replica_sum(per_gu)
    grad_dn = replica_sum(per_dn)
    returned = bring_back(jnp.where(is_learner, slot_dx, slot_fw), 1)
    mixing = jnp.where(is_learner, picker, weigher)
    base = jnp.where(is_learner, weight[:, None] * cot_wide, tokens.astype(jnp.float32))
    carried = (base + combine(mixing, returned)).astype(jnp.bfloat16)
    fresh_gu = renew(own_gu, grad_gu, 0, 0.5 / model_width**0.5)
    fresh_dn = renew(own_dn, grad_dn, 1, 0.5 / hidden_all**0.5)
    current = passed_along(carried, "grp", -1)
    picker, weigher = routing_tables(decode_experts[1], decode_gates[1], capacity, ep_count)
    (rows_got,) = spread([dispatch(picker, current)], 2)
    slot_out = forward_core(rows_got, fresh_gu, fresh_dn)
    returned = bring_back(slot_out, 3)
    current = (current.astype(jnp.float32) + combine(weigher, returned)).astype(jnp.bfloat16)
    final_rows = jnp.where(is_learner, carried, passed_along(current, "grp", 1))
    return final_rows[None]


def solution(mesh):
    placed = (
        P("grp", ("ep", "dp"), None),
        P(("ep", "dp"), None),
        P(),
        P(("ep", "dp"), None),
        P(("ep", "dp"), None),
        P(None, ("ep", "dp"), None),
        P(None, ("ep", "dp"), None),
        P("grp", "ep", None, None, "dp"),
        P("grp", "ep", "dp", None),
    )
    return jax.shard_map(
        per_device,
        mesh=mesh,
        in_specs=placed,
        out_specs=P("grp", ("ep", "dp"), None),
        check_vma=False,
    )
```

```python
import jax
import jax.numpy as jnp
from jax import lax
from jax.experimental import pallas as pl
from jax.experimental.pallas import tpu as pltpu
from jax.sharding import PartitionSpec as P
import functools

MESH = pl.DeviceIdType.MESH


def exchange_kernel(count, width, share, *refs):
    parts = len(refs) // 2 - 1
    sources, targets = refs[:parts], refs[parts:2 * parts]
    send_sem, recv_sem, own_sem = refs[2 * parts:]
    me = lax.axis_index("ep")
    rows = count * width
    side = lax.axis_index("dp")
    base = side * rows if share else 0
    barrier = pltpu.get_barrier_semaphore()

    def greet(k, carry):
        other = lax.rem(me + k, count)
        pl.semaphore_signal(barrier, inc=1, device_id={"ep": other}, device_id_type=MESH)
        return carry

    lax.fori_loop(1, count, greet, 0)
    if share:
        pl.semaphore_signal(barrier, inc=1, device_id={"dp": 1 - side}, device_id_type=MESH)
    pl.semaphore_wait(barrier, count - 1 + (1 if share else 0))

    def spot(index, start=0):
        return pl.ds(pl.multiple_of(start + index * width, width), width)

    owns = []
    for part in range(parts):
        own = pltpu.make_async_copy(
            sources[part].at[spot(me)], targets[part].at[spot(me, base)], own_sem.at[part, 0]
        )
        own.start()
        owns.append(own)

    def outgoing(part, k):
        step = jnp.where(k % 2 == 1, (k + 1) // 2, count - k // 2)
        other = lax.rem(me + step, count)
        return pltpu.make_async_remote_copy(
            src_ref=sources[part].at[spot(other)],
            dst_ref=targets[part].at[spot(me, base)],
            send_sem=send_sem.at[part, other],
            recv_sem=recv_sem.at[part, me],
            device_id={"ep": other},
            device_id_type=MESH,
        )

    def incoming(part, k):
        other = lax.rem(me + count - k, count)
        return pltpu.make_async_remote_copy(
            src_ref=sources[part].at[spot(other)],
            dst_ref=targets[part].at[spot(other, base)],
            send_sem=send_sem.at[part, other],
            recv_sem=recv_sem.at[part, other],
            device_id={"ep": other},
            device_id_type=MESH,
        )

    def launch(k, carry):
        for part in range(parts):
            outgoing(part, k).start()
        return carry

    lax.fori_loop(1, count, launch, 0)

    def settle(k, carry):
        for part in range(parts):
            outgoing(part, k).wait_send()
        return carry

    lax.fori_loop(1, count, settle, 0)

    def land(k, carry):
        for part in range(parts):
            incoming(part, k).wait_recv()
        return carry

    lax.fori_loop(1, count, land, 0)
    for own in owns:
        own.wait()
    if share:
        half = pl.ds(pl.multiple_of(base, rows), rows)
        yonder = pl.ds(pl.multiple_of((1 - side) * rows, rows), rows)
        passes = []
        for part in range(parts):
            onward = pltpu.make_async_remote_copy(
                src_ref=targets[part].at[half],
                dst_ref=targets[part].at[half],
                send_sem=own_sem.at[part, 1],
                recv_sem=own_sem.at[part, 2],
                device_id={"dp": 1 - side},
                device_id_type=MESH,
            )
            onward.start()
            passes.append(onward)
        for part in range(parts):
            passes[part].wait_send()
            pltpu.make_async_remote_copy(
                src_ref=targets[part].at[yonder],
                dst_ref=targets[part].at[yonder],
                send_sem=own_sem.at[part, 1],
                recv_sem=own_sem.at[part, 2],
                device_id={"dp": 1 - side},
                device_id_type=MESH,
            ).wait_recv()


def exchange(blocks, count, tag, share=False):
    parts = len(blocks)
    width = blocks[0].shape[0] // count
    grow = 2 if share else 1
    size = sum(block.size * block.dtype.itemsize for block in blocks)
    return pl.pallas_call(
        functools.partial(exchange_kernel, count, width, share),
        out_shape=[
            jax.ShapeDtypeStruct((grow * block.shape[0],) + block.shape[1:], block.dtype)
            for block in blocks
        ],
        in_specs=[pl.BlockSpec(memory_space=pl.ANY)] * parts,
        out_specs=[pl.BlockSpec(memory_space=pl.ANY)] * parts,
        scratch_shapes=[
            pltpu.SemaphoreType.DMA((parts, count)),
            pltpu.SemaphoreType.DMA((parts, count)),
            pltpu.SemaphoreType.DMA((parts, 3)),
        ],
        compiler_params=pltpu.CompilerParams(collective_id=tag, has_side_effects=True),
        cost_estimate=pl.CostEstimate(
            flops=0, transcendentals=0, bytes_accessed=(2 + 2 * grow) * size
        ),
    )(*blocks)


EPSILON = 1e-06


def passed_along(block, axis, distance):
    devices = range(lax.axis_size(axis))
    route = [(i - distance, i) for i in devices if i - distance in devices]
    return lax.ppermute(block, axis, route)


def routing_tables(expert_ids, gate_values, capacity, expert_count):
    row_count, top_count = expert_ids.shape
    flat_ids = expert_ids.reshape(row_count * top_count)
    onehot = (flat_ids[:, None] == jnp.arange(expert_count, dtype=jnp.int32)[None, :]).astype(
        jnp.int32
    )
    earlier = jnp.cumsum(onehot, axis=0) - onehot
    ranks = jnp.sum(earlier * onehot, axis=1)
    slots = flat_ids * capacity + ranks
    hits = (slots[:, None] == jnp.arange(expert_count * capacity, dtype=jnp.int32)[None, :]).astype(
        jnp.float32
    )
    hits = hits.reshape(row_count, top_count, expert_count * capacity)
    picker = jnp.sum(hits, axis=1)
    weigher = jnp.sum(hits * gate_values[:, :, None], axis=1)
    return (picker, weigher)


def replica_sum(per_replica):
    total = jnp.zeros(per_replica.shape[1:], jnp.float32)
    for replica in range(per_replica.shape[0]):
        total = total + per_replica[replica].astype(jnp.bfloat16).astype(jnp.float32)
    return total


def renew(weights, grads, axis_number, rate):
    scale = jnp.sqrt(jnp.mean(grads * grads, axis=axis_number, keepdims=True) + EPSILON)
    return (weights.astype(jnp.float32) - rate * grads / scale).astype(jnp.bfloat16)


def forward_core(slot_rows, weights_gu, weights_dn):
    hidden_count = weights_gu.shape[2]
    both = jnp.dot(
        slot_rows,
        weights_gu.reshape(slot_rows.shape[1], 2 * hidden_count),
        preferred_element_type=jnp.float32,
    ).reshape(-1, 2, hidden_count)
    active = both[:, 0]
    upward = both[:, 1]
    hidden = (active * jax.nn.sigmoid(active) * upward).astype(jnp.bfloat16)
    return jnp.dot(hidden, weights_dn, preferred_element_type=jnp.float32).astype(jnp.bfloat16)


def learn_core(slot_rows, slot_grads, weights_gu, weights_dn, rep_count):
    slot_count, model_width = slot_rows.shape
    hidden_count = weights_gu.shape[2]
    both = jnp.dot(
        slot_rows,
        weights_gu.reshape(model_width, 2 * hidden_count),
        preferred_element_type=jnp.float32,
    ).reshape(slot_count, 2, hidden_count)
    active = both[:, 0]
    upward = both[:, 1]
    sigma = jax.nn.sigmoid(active)
    swish = active * sigma
    hidden = (swish * upward).astype(jnp.bfloat16)
    back = lax.dot_general(
        slot_grads, weights_dn, (((1,), (1,)), ((), ())), preferred_element_type=jnp.float32
    )
    d_active = back * upward * sigma * (1.0 + active * (1.0 - sigma))
    d_upward = back * swish
    d_both = jnp.stack([d_active, d_upward], axis=1).astype(jnp.bfloat16)
    grad_dn = jnp.einsum(
        "pch,pcd->phd",
        hidden.reshape(rep_count, -1, hidden_count),
        slot_grads.reshape(rep_count, -1, model_width),
        preferred_element_type=jnp.float32,
    )
    grad_gu = jnp.einsum(
        "pcd,pcgh->pdgh",
        slot_rows.reshape(rep_count, -1, model_width),
        d_both.reshape(rep_count, -1, 2, hidden_count),
        preferred_element_type=jnp.float32,
    )
    slot_dx = jnp.einsum("mgh,dgh->md", d_both, weights_gu, preferred_element_type=jnp.float32)
    slot_fw = jnp.dot(hidden, weights_dn, preferred_element_type=jnp.float32)
    return (grad_gu, grad_dn, slot_dx.astype(jnp.bfloat16), slot_fw.astype(jnp.bfloat16))


def per_device(
    rows_in,
    cotangent,
    lengths,
    train_experts,
    train_gates,
    decode_experts,
    decode_gates,
    gate_up,
    down,
):
    ep_count = lax.axis_size("ep")
    dp_count = lax.axis_size("dp")
    row_count, model_width = cotangent.shape
    top_count = train_experts.shape[1]
    capacity = min(row_count, max(2, 4 * row_count * top_count // (3 * ep_count)))
    is_learner = lax.axis_index("grp") == 0
    own_gu = gate_up[0, 0]
    own_dn = down[0, 0]
    hidden_all = own_gu.shape[2] * dp_count

    def spread(buffers, tag):
        return exchange(buffers, ep_count, tag, share=True)

    def bring_back(pieces, tag):
        half = pieces.shape[0] // dp_count
        mine = lax.axis_index("dp")
        keep = lax.dynamic_slice_in_dim(pieces, mine * half, half)
        give = lax.dynamic_slice_in_dim(pieces, (1 - mine) * half, half)
        got = lax.ppermute(give, "dp", [(0, 1), (1, 0)])
        summed = (keep.astype(jnp.float32) + got.astype(jnp.float32)).astype(jnp.bfloat16)
        return exchange([summed], ep_count, tag)[0]

    def combine(mixing, returned):
        total = returned.astype(jnp.float32)
        return jnp.einsum("rs,sd->rd", mixing, total, precision=lax.Precision.HIGHEST)

    def dispatch(picker, values):
        buffer = jnp.einsum(
            "rs,rd->sd", picker.astype(jnp.bfloat16), values, preferred_element_type=jnp.float32
        )
        return buffer.astype(jnp.bfloat16)

    tokens = rows_in[0]
    total_rows = row_count * ep_count * dp_count
    longest = 2 * total_rows // lengths.shape[0]
    first_row = (lax.axis_index("ep") * dp_count + lax.axis_index("dp")) * row_count
    places = first_row + jnp.arange(row_count, dtype=jnp.int32)
    ends = jnp.cumsum(lengths)
    starts = ends - lengths
    inside = (places[:, None] >= starts[None, :]) & (places[:, None] < ends[None, :])
    seq_len = jnp.sum(jnp.where(inside, lengths[None, :], 0), axis=1).astype(jnp.float32)
    weight = 2.0 * longest / (seq_len + longest)
    route_ids = jnp.where(is_learner, train_experts, decode_experts[0])
    route_gates = jnp.where(is_learner, train_gates, decode_gates[0])
    picker, weigher = routing_tables(route_ids, route_gates, capacity, ep_count)
    row_buffer = dispatch(picker, tokens)
    cot_wide = cotangent.astype(jnp.float32)
    grad_buffer = jnp.einsum(
        "rs,rd->sd", weigher * weight[:, None], cot_wide, precision=lax.Precision.HIGHEST
    ).astype(jnp.bfloat16)
    rows_got, grads_got = spread([row_buffer, grad_buffer], 0)
    per_gu, per_dn, slot_dx, slot_fw = learn_core(rows_got, grads_got, own_gu, own_dn, dp_count)
    grad_gu = replica_sum(per_gu)
    grad_dn = replica_sum(per_dn)
    returned = bring_back(jnp.where(is_learner, slot_dx, slot_fw), 1)
    mixing = jnp.where(is_learner, picker, weigher)
    base = jnp.where(is_learner, weight[:, None] * cot_wide, tokens.astype(jnp.float32))
    carried = (base + combine(mixing, returned)).astype(jnp.bfloat16)
    fresh_gu = renew(own_gu, grad_gu, 0, 0.5 / model_width**0.5)
    fresh_dn = renew(own_dn, grad_dn, 1, 0.5 / hidden_all**0.5)
    current = passed_along(carried, "grp", -1)
    picker, weigher = routing_tables(decode_experts[1], decode_gates[1], capacity, ep_count)
    (rows_got,) = spread([dispatch(picker, current)], 2)
    slot_out = forward_core(rows_got, fresh_gu, fresh_dn)
    returned = bring_back(slot_out, 3)
    current = (current.astype(jnp.float32) + combine(weigher, returned)).astype(jnp.bfloat16)
    final_rows = jnp.where(is_learner, carried, passed_along(current, "grp", 1))
    return final_rows[None]


def solution(mesh):
    placed = (
        P("grp", ("ep", "dp"), None),
        P(("ep", "dp"), None),
        P(),
        P(("ep", "dp"), None),
        P(("ep", "dp"), None),
        P(None, ("ep", "dp"), None),
        P(None, ("ep", "dp"), None),
        P("grp", "ep", None, None, "dp"),
        P("grp", "ep", "dp", None),
    )
    return jax.shard_map(
        per_device,
        mesh=mesh,
        in_specs=placed,
        out_specs=P("grp", ("ep", "dp"), None),
        check_vma=False,
    )
```
